512 devices in a mesh: dom: 16 (over y, core), aux: 32 (over x, z).
Axes of the slice: x: 4, y: 8, z: 8, core: 2. Of those that a mesh axis runs over, the one named last changes fastest.
Arguments:
- integrals: bfloat16 [16, 1024, 512, 128], P('dom', 'aux'), may hold values from -0.25 to 0.25
- density: bfloat16 [16, 4, 128, 128], P('dom'), may hold values from -0.25 to 0.25
- dens_cols: int32 [16, 4], replicated, may hold values from 0 to 15, as said below
- neighbours: int32 [16, 4], replicated, may hold values from 0 to 15, as said below
- metric: bfloat16 [16, 1024, 1024], P('dom', 'aux'), may hold values from -0.5 to 2.5, as said below
Outputs:
- exchange: float32 [16, 128, 128], P('dom')
The draws below stay inside these ranges and needn't reach their ends.
Inputs may be any that keep to these rules, and one draw needn't show every extreme that they name: `neighbours`: in each row the entries are distinct; position 0 holds the row's own block, the others are blocks within cyclic distance 2 of it, both blocks at distance 1 among them. `dens_cols`: in each row the entries are distinct; position 0 holds the row's own block, the others are blocks within cyclic distance 2 of it, both blocks at distance 1 among them. `metric`: each domain's matrix is symmetric.
All inputs are finite; a program needn't handle non-finite values.
Results may differ from the reference program's by a relative error of at most 0.004.
Values may be sent and summed in bfloat16 or wider, within the bound.
No kernel may reach another device: no remote copies, remote signals or barrier semaphores. Data moves between devices by JAX's collectives and lax.ppermute only.
A program may use at most 64 MiB of HBM per device.

```python
import jax
import jax.numpy as jnp
from jax import lax

BS = 128
NAUX = 1024
NEI = 4
DT = 4
N_DOM = 16


def near_blocks(key, count):
    candidates = jnp.arange(1, N_DOM, dtype=jnp.int32)
    distance = jnp.minimum(candidates, N_DOM - candidates)
    jitter = jax.random.randint(key, (N_DOM, N_DOM - 1), 0, 1024, dtype=jnp.int32)
    scores = (distance[None, :] * 2048 + jitter) * N_DOM + candidates[None, :]
    unused, chosen_index = lax.top_k(-scores, count - 1)
    chosen = jnp.take(candidates, chosen_index)
    offsets = jnp.concatenate([jnp.zeros((N_DOM, 1), jnp.int32), chosen], axis=1)
    return ((jnp.arange(N_DOM, dtype=jnp.int32)[:, None] + offsets) % N_DOM).astype(jnp.int32)


def draw_neighbours(key, part):
    return near_blocks(jax.random.fold_in(key, 11), NEI)


def draw_dens_cols(key, part):
    return near_blocks(jax.random.fold_in(key, 23), DT)


def draw_metric(key, part):
    key_diag = jax.random.fold_in(key, 37)
    key_off = jax.random.fold_in(key, 41)
    diagonal = jnp.exp(jax.random.uniform(key_diag, (N_DOM, NAUX), jnp.float32, jnp.log(0.5), jnp.log(2.0)))
    off_diag = jax.random.truncated_normal(key_off, -4.0, 4.0, (N_DOM, NAUX, NAUX), jnp.float32)
    off_diag = off_diag * (0.5 / jnp.sqrt(jnp.float32(NAUX)))
    symmetric = (off_diag + jnp.swapaxes(off_diag, 1, 2)) * 0.7071
    return (symmetric + diagonal[:, :, None] * jnp.eye(NAUX, dtype=jnp.float32)[None]).astype(jnp.bfloat16)


def block_scale(own_key, extent, split, least, top_value):
    level, own = 1.0, jax.random.fold_in(own_key, 6)
    for dim, parts in split:
        draws = jnp.exp(jax.random.uniform(jax.random.fold_in(own, dim), (parts,), jnp.float32, least / len(split), top_value / len(split)))
        level = level * jnp.repeat(draws, extent[dim] // parts).reshape([-1 if axis == dim else 1 for axis in range(len(extent))])
    return level


def scatter_about(key, dims, scale, bound, split=(), kind=jnp.bfloat16):
    drawn = jax.random.normal(key, dims, jnp.float32) * scale
    if len(split) > 0:
        drawn = block_scale(key, dims, split, -0.22, 0.18) * drawn
    return jnp.clip(drawn, min=-bound, max=bound).astype(kind)


def setup_inputs(seed: int = 0) -> dict:
    arg_keys = jax.random.split(jax.random.key(seed), 6)
    integrals = scatter_about(arg_keys[0], (N_DOM, NAUX, NEI * BS, BS), (NEI * BS) ** -0.5, 0.25, ((0, 16), (1, 32)))
    density = scatter_about(arg_keys[1], (N_DOM, DT, BS, BS), (NEI * BS) ** -0.5, 0.25, ((0, 16),))
    dens_cols = draw_dens_cols(jax.random.fold_in(arg_keys[5], 71), 0)
    neighbours = draw_neighbours(jax.random.fold_in(arg_keys[5], 71), 0)
    metric = draw_metric(jax.random.fold_in(arg_keys[5], 71), 0)
    return {"integrals": integrals, "density": density, "dens_cols": dens_cols, "neighbours": neighbours, "metric": metric}


def local_density(listed_blocks, density, dens_cols):
    picked = jnp.take(density, listed_blocks, axis=0).astype(jnp.float32)
    tile_cols = jnp.take(dens_cols, listed_blocks, axis=0)
    matches = (tile_cols[:, None, :] == listed_blocks[None, :, None]).astype(jnp.float32)
    dense_tiles = jnp.einsum("jsk,jkab->jasb", matches, picked)
    return dense_tiles.reshape(NEI * BS, NEI * BS)


def reference(integrals, density, dens_cols, neighbours, metric):
    def one_domain(domain_items):
        integral_tile, metric_rows, listed_blocks = domain_items
        density_local = local_density(listed_blocks, density, dens_cols)
        wide_ints = integral_tile.astype(jnp.float32)
        half_product = jnp.einsum("ls,plm->psm", density_local, wide_ints).astype(jnp.bfloat16)
        fitted = jnp.einsum("qp,psm->qsm", metric_rows.astype(jnp.float32), wide_ints).astype(jnp.bfloat16)
        return jnp.einsum("psm,psn->mn", half_product.astype(jnp.float32), fitted.astype(jnp.float32))

    return lax.map(one_domain, (integrals, metric, neighbours))
```

```python
import jax
import jax.numpy as jnp
from jax import lax
from jax.experimental import pallas as pl
from jax.experimental.pallas import tpu as pltpu
from jax.sharding import PartitionSpec as P

RAD = 2
X_LEN = 4


def passed_along(block, axis, distance):
    devices = range(lax.axis_size(axis))
    route = [((i - distance) % len(devices), i) for i in devices]
    return lax.ppermute(block, axis, route)


def from_grid(block, dx, dz):
    z_len = lax.axis_size("aux") // X_LEN
    route = []
    for x in range(X_LEN):
        for z in range(z_len):
            source = ((x - dx) % X_LEN) * z_len + (z - dz) % z_len
            route.append((source, x * z_len + z))
    return lax.ppermute(block, "aux", route)


def in_order(pieces, here):
    count = len(pieces)
    stack = jnp.stack([pieces[(-k) % count] for k in range(count)])
    twice = jnp.concatenate([stack, stack])
    return lax.dynamic_slice_in_dim(twice, (count - here) % count, count, 0)


def gathered_metric(rows):
    z_len = lax.axis_size("aux") // X_LEN
    me = lax.axis_index("aux")
    my_x, my_z = me // z_len, me % z_len
    up, down = {0: rows}, {0: rows}
    for k in range(1, z_len // 2 + 1):
        up[k] = from_grid(up[k - 1], 0, 1)
        if k < z_len // 2:
            down[k] = from_grid(down[k - 1], 0, -1)
    pieces = [up[k] if k <= z_len // 2 else down[z_len - k] for k in range(z_len)]
    line = in_order(pieces, my_z).reshape(z_len * rows.shape[0], rows.shape[1])
    sides = [line, from_grid(line, 1, 0), from_grid(line, 2, 0), from_grid(line, 3, 0)]
    return in_order(sides, my_x).reshape(-1, rows.shape[1])


def fit_kernel(metric_ref, ints_ref, out_ref):
    parts, width, depth, cols = ints_ref.shape
    for w in range(width):
        right = ints_ref[:, w].reshape(parts * depth, cols)
        out_ref[w] = lax.dot_general(
            right, metric_ref[...], (((0,), (1,)), ((), ())),
            preferred_element_type=jnp.float32,
        ).astype(out_ref.dtype)


def fit(metric, ints):
    parts, slots, depth, cols = ints.shape
    width = 2
    rows = parts * depth
    return pl.pallas_call(
        fit_kernel,
        out_shape=jax.ShapeDtypeStruct((slots, cols, rows), ints.dtype),
        grid=(slots // width,),
        in_specs=[
            pl.BlockSpec((rows, rows), lambda i: (0, 0)),
            pl.BlockSpec((parts, width, depth, cols), lambda i: (0, i, 0, 0)),
        ],
        out_specs=pl.BlockSpec((width, cols, rows), lambda i: (i, 0, 0)),
        compiler_params=pltpu.CompilerParams(vmem_limit_bytes=24 << 20),
        cost_estimate=pl.CostEstimate(
            flops=2 * rows * rows * slots * cols,
            bytes_accessed=2 * rows * rows + 4 * rows * slots * cols,
            transcendentals=0,
        ),
    )(metric, ints)


def close_kernel(fitted_ref, half_ref, out_ref, total_ref):
    step = pl.program_id(0)
    parts, width, depth, cols = half_ref.shape

    @pl.when(step == 0)
    def _():
        total_ref[...] = jnp.zeros_like(total_ref)

    total = total_ref[...]
    for w in range(width):
        right = half_ref[:, w].reshape(parts * depth, cols)
        total += jnp.dot(fitted_ref[w], right, preferred_element_type=jnp.float32)
    total_ref[...] = total

    @pl.when(step == pl.num_programs(0) - 1)
    def _():
        out_ref[...] = total_ref[...].T


def close(fitted, half):
    parts, slots, depth, cols = half.shape
    width = 4
    rows = parts * depth
    return pl.pallas_call(
        close_kernel,
        out_shape=jax.ShapeDtypeStruct((cols, cols), jnp.float32),
        grid=(slots // width,),
        in_specs=[
            pl.BlockSpec((width, cols, rows), lambda i: (i, 0, 0)),
            pl.BlockSpec((parts, width, depth, cols), lambda i: (0, i, 0, 0)),
        ],
        out_specs=pl.BlockSpec((cols, cols), lambda i: (0, 0)),
        scratch_shapes=[pltpu.VMEM((cols, cols), jnp.float32)],
        compiler_params=pltpu.CompilerParams(vmem_limit_bytes=24 << 20),
        cost_estimate=pl.CostEstimate(
            flops=2 * rows * slots * cols * cols,
            bytes_accessed=4 * rows * slots * cols,
            transcendentals=0,
        ),
    )(fitted, half)


def local_density(density, dens_cols, neighbours):
    domain_count = lax.axis_size("dom")
    my_domain = lax.axis_index("dom")
    block_size = density.shape[2]
    neigh_count = neighbours.shape[1]
    my_blocks = lax.dynamic_index_in_dim(neighbours, my_domain, 0, keepdims=False)
    slabs = []
    for offset in range(-RAD, RAD + 1):
        slabs.append(density[0] if offset == 0 else passed_along(density, "dom", -offset)[0])
    row_slabs = jnp.stack(slabs)
    slot_index = (my_blocks - my_domain + RAD) % domain_count
    picked = jnp.take(row_slabs, slot_index, axis=0)
    tile_cols = jnp.take(dens_cols, my_blocks, axis=0)
    matches = (tile_cols[:, None, :] == my_blocks[None, :, None]).astype(jnp.bfloat16)
    tiles = jnp.einsum("jsk,jkab->jasb", matches, picked, preferred_element_type=jnp.float32)
    order = neigh_count * block_size
    return tiles.astype(jnp.bfloat16).reshape(order, order)


def exchanged(array):
    group = lax.axis_size("aux")
    count, slots, cols = array.shape
    by_slot = array.transpose(1, 0, 2).reshape(group, slots // group, count, cols)
    return lax.all_to_all(by_slot, "aux", split_axis=0, concat_axis=0, tiled=True)


def summed(partial):
    group = lax.axis_size("aux")
    rows, cols = partial.shape
    slices = partial.reshape(group, rows // group, cols)
    parts = lax.all_to_all(slices, "aux", split_axis=0, concat_axis=0, tiled=True)
    mine = jnp.sum(parts, axis=0)
    copies = jnp.broadcast_to(mine[None], slices.shape)
    whole = lax.all_to_all(copies, "aux", split_axis=0, concat_axis=0, tiled=True)
    return whole.reshape(rows, cols)


def body(integrals, density, dens_cols, neighbours, metric):
    ints = integrals[0]
    ints_moved = exchanged(ints)
    dense = local_density(density, dens_cols, neighbours)
    half = jnp.einsum("ls,plm->psm", dense, ints, preferred_element_type=jnp.float32)
    half_moved = exchanged(half.astype(jnp.bfloat16))
    fitted = fit(gathered_metric(metric[0]), ints_moved)
    partial = close(fitted, half_moved)
    return summed(partial)[None]


def solution(mesh):
    return jax.shard_map(
        body,
        mesh=mesh,
        in_specs=(
            P("dom", "aux", None, None),
            P("dom", None, None, None),
            P(),
            P(),
            P("dom", "aux", None),
        ),
        out_specs=P("dom", None, None),
        check_vma=False,
    )
```

```python
import jax
import jax.numpy as jnp
from jax import lax
from jax.experimental import pallas as pl
from jax.experimental.pallas import tpu as pltpu
from jax.sharding import PartitionSpec as P


RAD = 2
X_LEN = 4


def passed_along(block, axis, distance):
    devices = range(lax.axis_size(axis))
    route = [((i - distance) % len(devices), i) for i in devices]
    return lax.ppermute(block, axis, route)


def from_x(block, distance):
    count = lax.axis_size("aux")
    z_len = count // X_LEN
    route = [((i - distance * z_len) % count, i) for i in range(count)]
    return lax.ppermute(block, "aux", route)


def groups_along(which):
    z_len = lax.axis_size("aux") // X_LEN
    lines = [[x * z_len + z for z in range(z_len)] for x in range(X_LEN)]
    return lines if which == "z" else [list(line) for line in zip(*lines)]


def to_all(copies, which):
    return lax.all_to_all(
        copies, "aux", split_axis=0, concat_axis=0, tiled=True,
        axis_index_groups=groups_along(which),
    )


def fit_kernel(x_ref, *refs):
    *metric_refs, ints_ref, out_ref = refs
    parts, width, depth, cols = ints_ref.shape
    count = len(metric_refs)
    for w in range(width):
        right = ints_ref[:, w].reshape(parts * depth, cols)
        for k, metric_ref in enumerate(metric_refs):
            rows = metric_ref.shape[0]
            place = lax.rem(x_ref[0] + (count - k), count)
            start = pl.multiple_of(place * rows, rows)
            out_ref[w, :, pl.ds(start, rows)] = lax.dot_general(
                right, metric_ref[...], (((0,), (1,)), ((), ())),
                preferred_element_type=jnp.float32,
            ).astype(out_ref.dtype)


def fit(metric_parts, my_x, ints):
    parts, slots, depth, cols = ints.shape
    width = 2
    rows = parts * depth
    metric_spec = pl.BlockSpec(metric_parts[0].shape, lambda i, x: (0, 0))
    return pl.pallas_call(
        fit_kernel,
        out_shape=jax.ShapeDtypeStruct((slots, cols, rows), ints.dtype),
        grid_spec=pltpu.PrefetchScalarGridSpec(
            num_scalar_prefetch=1,
            grid=(slots // width,),
            in_specs=[metric_spec] * len(metric_parts) + [
                pl.BlockSpec((parts, width, depth, cols), lambda i, x: (0, i, 0, 0)),
            ],
            out_specs=pl.BlockSpec((width, cols, rows), lambda i, x: (i, 0, 0)),
        ),
        compiler_params=pltpu.CompilerParams(vmem_limit_bytes=24 << 20),
        cost_estimate=pl.CostEstimate(
            flops=2 * rows * rows * slots * cols,
            bytes_accessed=2 * rows * rows + 4 * rows * slots * cols,
            transcendentals=0,
        ),
    )(my_x, *metric_parts, ints)


def close_kernel(fitted_ref, half_ref, out_ref, total_ref):
    step = pl.program_id(0)
    parts, width, depth, cols = half_ref.shape

    @pl.when(step == 0)
    def _():
        total_ref[...] = jnp.zeros_like(total_ref)

    total = total_ref[...]
    for w in range(width):
        right = half_ref[:, w].reshape(parts * depth, cols)
        total += jnp.dot(fitted_ref[w], right, preferred_element_type=jnp.float32)
    total_ref[...] = total

    @pl.when(step == pl.num_programs(0) - 1)
    def _():
        done = total_ref[...].T
        for k in range(out_ref.shape[0]):
            out_ref[k] = done


def close(fitted, half):
    parts, slots, depth, cols = half.shape
    width = 4
    rows = parts * depth
    return pl.pallas_call(
        close_kernel,
        out_shape=jax.ShapeDtypeStruct((X_LEN, cols, cols), jnp.float32),
        grid=(slots // width,),
        in_specs=[
            pl.BlockSpec((width, cols, rows), lambda i: (i, 0, 0)),
            pl.BlockSpec((parts, width, depth, cols), lambda i: (0, i, 0, 0)),
        ],
        out_specs=pl.BlockSpec((X_LEN, cols, cols), lambda i: (0, 0, 0)),
        scratch_shapes=[pltpu.VMEM((cols, cols), jnp.float32)],
        compiler_params=pltpu.CompilerParams(vmem_limit_bytes=24 << 20),
        cost_estimate=pl.CostEstimate(
            flops=2 * rows * slots * cols * cols,
            bytes_accessed=4 * rows * slots * cols,
            transcendentals=0,
        ),
    )(fitted, half)


def local_density(density, dens_cols, neighbours):
    domain_count = lax.axis_size("dom")
    my_domain = lax.axis_index("dom")
    block_size = density.shape[2]
    neigh_count = neighbours.shape[1]
    my_blocks = lax.dynamic_index_in_dim(neighbours, my_domain, 0, keepdims=False)
    slabs = []
    for offset in range(-RAD, RAD + 1):
        slabs.append(density[0] if offset == 0 else passed_along(density, "dom", -offset)[0])
    row_slabs = jnp.stack(slabs)
    slot_index = (my_blocks - my_domain + RAD) % domain_count
    picked = jnp.take(row_slabs, slot_index, axis=0)
    tile_cols = jnp.take(dens_cols, my_blocks, axis=0)
    matches = (tile_cols[:, None, :] == my_blocks[None, :, None]).astype(jnp.bfloat16)
    tiles = jnp.einsum("jsk,jkab->jasb", matches, picked, preferred_element_type=jnp.float32)
    order = neigh_count * block_size
    return tiles.astype(jnp.bfloat16).reshape(order, order)


def by_slot(array):
    group = lax.axis_size("aux")
    count, slots, cols = array.shape
    return array.transpose(1, 0, 2).reshape(group, slots // group, count, cols)


def exchanged(array):
    return lax.all_to_all(array, "aux", split_axis=0, concat_axis=0, tiled=True)


def body(integrals, density, dens_cols, neighbours, metric):
    ints, rows = integrals[0], metric[0]
    group = lax.axis_size("aux")
    z_len = group // X_LEN
    cols = ints.shape[2]
    line = to_all(jnp.broadcast_to(rows[None], (z_len, *rows.shape)), "z")
    line = line.reshape(z_len * rows.shape[0], rows.shape[1])
    line, ints_out = lax.optimization_barrier((line, by_slot(ints)))
    ints_moved = exchanged(ints_out)
    sides = [line] + [from_x(line, k) for k in range(1, X_LEN)]
    dense = local_density(density, dens_cols, neighbours)
    half = jnp.einsum("ls,plm->psm", dense, ints, preferred_element_type=jnp.float32)
    half_moved = exchanged(by_slot(half.astype(jnp.bfloat16)))
    starts = jnp.arange(1, X_LEN, dtype=jnp.int32) * z_len
    my_x = jnp.sum(starts <= lax.axis_index("aux"), dtype=jnp.int32)[None]
    fitted = fit(sides, my_x, ints_moved)
    shares = close(fitted, half_moved)
    shares = jnp.sum(to_all(shares, "x"), axis=0)
    shares = jnp.broadcast_to(shares[None], (z_len, cols, cols))
    return jnp.sum(to_all(shares, "z"), axis=0)[None]


def solution(mesh):
    return jax.shard_map(
        body,
        mesh=mesh,
        in_specs=(
            P("dom", "aux", None, None),
            P("dom", None, None, None),
            P(),
            P(),
            P("dom", "aux", None),
        ),
        out_specs=P("dom", None, None),
        check_vma=False,
    )
```

```python
import jax
import jax.numpy as jnp
from jax import lax
from jax.experimental import pallas as pl
from jax.experimental.pallas import tpu as pltpu
from jax.sharding import PartitionSpec as P


RAD = 2
X_LEN = 4


def passed_along(block, axis, distance):
    devices = range(lax.axis_size(axis))
    route = [((i - distance) % len(devices), i) for i in devices]
    return lax.ppermute(block, axis, route)


def from_x(block, distance):
    count = lax.axis_size("aux")
    z_len = count // X_LEN
    route = [((i - distance * z_len) % count, i) for i in range(count)]
    return lax.ppermute(block, "aux", route)


def groups_along(which):
    z_len = lax.axis_size("aux") // X_LEN
    lines = [[x * z_len + z for z in range(z_len)] for x in range(X_LEN)]
    return lines if which == "z" else [list(line) for line in zip(*lines)]


def to_all(copies, which):
    return lax.all_to_all(
        copies, "aux", split_axis=0, concat_axis=0, tiled=True,
        axis_index_groups=groups_along(which),
    )


BLOCKS = {
    (0, 0): (0, 0), (0, 1): (0, 1), (0, 2): (0, 2),
    (1, 1): (1, 0), (1, 2): (1, 1), (1, 3): (1, 2),
    (2, 2): (2, 0), (2, 3): (2, 1),
    (3, 3): (3, 0), (3, 0): (3, 1),
}


def fit_kernel(x_ref, *refs):
    *metric_refs, ints_ref, out_ref = refs
    parts, width, depth, cols = ints_ref.shape
    count = len(metric_refs)
    share = parts // count
    block = share * depth
    columns = []
    for k in range(count):
        place = lax.rem(x_ref[0] + k, count)
        tile = ints_ref[pl.ds(pl.multiple_of(place * share, share), share)]
        columns.append(jnp.concatenate(
            [tile[:, w].reshape(block, cols).T for w in range(width)], axis=0
        ))
    for q in range(count):
        total = jnp.zeros((width * cols, block), jnp.float32)
        for p in range(count):
            stored = (q, p) in BLOCKS
            piece, place = BLOCKS[(q, p) if stored else (p, q)]
            right = metric_refs[piece][:, place * block:(place + 1) * block]
            total += lax.dot_general(
                columns[p], right, (((1,), (1 if stored else 0,)), ((), ())),
                preferred_element_type=jnp.float32,
            )
        total = total.astype(out_ref.dtype)
        place = lax.rem(x_ref[0] + q, count)
        for w in range(width):
            out_ref[w, :, pl.ds(pl.multiple_of(place * block, block), block)] = (
                total[w * cols:(w + 1) * cols]
            )


def fit(metric_parts, my_x, ints):
    parts, slots, depth, cols = ints.shape
    width = 2
    rows = parts * depth
    return pl.pallas_call(
        fit_kernel,
        out_shape=jax.ShapeDtypeStruct((slots, cols, rows), ints.dtype),
        grid_spec=pltpu.PrefetchScalarGridSpec(
            num_scalar_prefetch=1,
            grid=(slots // width,),
            in_specs=[
                pl.BlockSpec(part.shape, lambda i, x: (0, 0)) for part in metric_parts
            ] + [
                pl.BlockSpec((parts, width, depth, cols), lambda i, x: (0, i, 0, 0)),
            ],
            out_specs=pl.BlockSpec((width, cols, rows), lambda i, x: (i, 0, 0)),
        ),
        compiler_params=pltpu.CompilerParams(vmem_limit_bytes=24 << 20),
        cost_estimate=pl.CostEstimate(
            flops=2 * rows * rows * slots * cols,
            bytes_accessed=2 * rows * rows + 4 * rows * slots * cols,
            transcendentals=0,
        ),
    )(my_x, *metric_parts, ints)


def close_kernel(fitted_ref, half_ref, out_ref, total_ref):
    step = pl.program_id(0)
    parts, width, depth, cols = half_ref.shape

    @pl.when(step == 0)
    def _():
        total_ref[...] = jnp.zeros_like(total_ref)

    total = total_ref[...]
    for w in range(width):
        right = half_ref[:, w].reshape(parts * depth, cols)
        total += jnp.dot(fitted_ref[w], right, preferred_element_type=jnp.float32)
    total_ref[...] = total

    @pl.when(step == pl.num_programs(0) - 1)
    def _():
        done = total_ref[...].T
        for k in range(out_ref.shape[0]):
            out_ref[k] = done


def close(fitted, half):
    parts, slots, depth, cols = half.shape
    width = 4
    rows = parts * depth
    return pl.pallas_call(
        close_kernel,
        out_shape=jax.ShapeDtypeStruct((X_LEN, cols, cols), jnp.float32),
        grid=(slots // width,),
        in_specs=[
            pl.BlockSpec((width, cols, rows), lambda i: (i, 0, 0)),
            pl.BlockSpec((parts, width, depth, cols), lambda i: (0, i, 0, 0)),
        ],
        out_specs=pl.BlockSpec((X_LEN, cols, cols), lambda i: (0, 0, 0)),
        scratch_shapes=[pltpu.VMEM((cols, cols), jnp.float32)],
        compiler_params=pltpu.CompilerParams(vmem_limit_bytes=24 << 20),
        cost_estimate=pl.CostEstimate(
            flops=2 * rows * slots * cols * cols,
            bytes_accessed=4 * rows * slots * cols,
            transcendentals=0,
        ),
    )(fitted, half)


def local_density(density, dens_cols, neighbours):
    domain_count = lax.axis_size("dom")
    my_domain = lax.axis_index("dom")
    block_size = density.shape[2]
    neigh_count = neighbours.shape[1]
    my_blocks = lax.dynamic_index_in_dim(neighbours, my_domain, 0, keepdims=False)
    slabs = []
    for offset in range(-RAD, RAD + 1):
        slabs.append(density[0] if offset == 0 else passed_along(density, "dom", -offset)[0])
    row_slabs = jnp.stack(slabs)
    slot_index = (my_blocks - my_domain + RAD) % domain_count
    picked = jnp.take(row_slabs, slot_index, axis=0)
    tile_cols = jnp.take(dens_cols, my_blocks, axis=0)
    matches = (tile_cols[:, None, :] == my_blocks[None, :, None]).astype(jnp.bfloat16)
    tiles = jnp.einsum("jsk,jkab->jasb", matches, picked, preferred_element_type=jnp.float32)
    order = neigh_count * block_size
    return tiles.astype(jnp.bfloat16).reshape(order, order)


def by_slot(array):
    group = lax.axis_size("aux")
    count, slots, cols = array.shape
    return array.transpose(1, 0, 2).reshape(group, slots // group, count, cols)


def exchanged(array):
    return lax.all_to_all(array, "aux", split_axis=0, concat_axis=0, tiled=True)


def body(integrals, density, dens_cols, neighbours, metric):
    ints, rows = integrals[0], metric[0]
    group = lax.axis_size("aux")
    z_len = group // X_LEN
    cols = ints.shape[2]
    starts = jnp.arange(1, X_LEN, dtype=jnp.int32) * z_len
    my_x = jnp.sum(starts <= lax.axis_index("aux"), dtype=jnp.int32)
    side = rows.shape[1] // X_LEN
    around = jnp.concatenate([rows, rows[:, :2 * side]], axis=1)
    kept = lax.dynamic_slice_in_dim(around, my_x * side, 3 * side, 1)
    line = to_all(jnp.broadcast_to(kept[None], (z_len, *kept.shape)), "z")
    line = line.reshape(z_len * kept.shape[0], kept.shape[1])
    line, ints_out = lax.optimization_barrier((line, by_slot(ints)))
    ints_moved = exchanged(ints_out)
    short = line[:, :2 * side]
    parts = [line, from_x(line, -1), from_x(short, 2), from_x(short, 1)]
    dense = local_density(density, dens_cols, neighbours)
    half = jnp.einsum("ls,plm->psm", dense, ints, preferred_element_type=jnp.float32)
    half_moved = exchanged(by_slot(half.astype(jnp.bfloat16)))
    fitted = fit(parts, my_x[None], ints_moved)
    shares = close(fitted, half_moved)
    shares = jnp.sum(to_all(shares, "x"), axis=0)
    shares = jnp.broadcast_to(shares[None], (z_len, cols, cols))
    return jnp.sum(to_all(shares, "z"), axis=0)[None]


def solution(mesh):
    return jax.shard_map(
        body,
        mesh=mesh,
        in_specs=(
            P("dom", "aux", None, None),
            P("dom", None, None, None),
            P(),
            P(),
            P("dom", "aux", None),
        ),
        out_specs=P("dom", None, None),
        check_vma=False,
    )
```

```python
import jax
import jax.numpy as jnp
from jax import lax
from jax.experimental import pallas as pl
from jax.experimental.pallas import tpu as pltpu
from jax.sharding import PartitionSpec as P


RAD = 2
X_LEN = 4


def passed_along(block, axis, distance):
    devices = range(lax.axis_size(axis))
    route = [((i - distance) % len(devices), i) for i in devices]
    return lax.ppermute(block, axis, route)


def from_x(block, distance):
    count = lax.axis_size("aux")
    z_len = count // X_LEN
    route = [((i - distance * z_len) % count, i) for i in range(count)]
    return lax.ppermute(block, "aux", route)


def groups_along(which):
    z_len = lax.axis_size("aux") // X_LEN
    lines = [[x * z_len + z for z in range(z_len)] for x in range(X_LEN)]
    return lines if which == "z" else [list(line) for line in zip(*lines)]


def to_all(copies, which):
    return lax.all_to_all(
        copies, "aux", split_axis=0, concat_axis=0, tiled=True,
        axis_index_groups=groups_along(which),
    )


def metric_kernel(me_ref, rows_ref, out_ref):
    copies, _, kept = out_ref.shape
    side = rows_ref.shape[1] // X_LEN
    my_x = me_ref[0] // copies
    for k in range(kept // side):
        place = lax.rem(my_x + k, X_LEN)
        block = rows_ref[:, pl.ds(pl.multiple_of(place * side, side), side)]
        for copy in range(copies):
            out_ref[copy, :, k * side:(k + 1) * side] = block


def metric_copies(rows, me, copies):
    count, cols = rows.shape
    return pl.pallas_call(
        metric_kernel,
        out_shape=jax.ShapeDtypeStruct((copies, count, 3 * cols // X_LEN), rows.dtype),
        in_specs=[
            pl.BlockSpec(memory_space=pltpu.SMEM),
            pl.BlockSpec(memory_space=pltpu.VMEM),
        ],
        out_specs=pl.BlockSpec(memory_space=pltpu.VMEM),
        compiler_params=pltpu.CompilerParams(vmem_limit_bytes=4 << 20),
    )(me, rows)


BLOCKS = {
    (0, 0): (0, 0), (0, 1): (0, 1), (0, 2): (0, 2),
    (1, 1): (1, 0), (1, 2): (1, 1), (1, 3): (1, 2),
    (2, 2): (2, 0), (2, 3): (2, 1),
    (3, 3): (3, 0), (3, 0): (3, 1),
}


def fit_kernel(me_ref, *refs):
    *metric_refs, ints_ref, out_ref = refs
    parts, width, depth, cols = ints_ref.shape
    count = len(metric_refs)
    share = parts // count
    block = share * depth
    my_x = me_ref[0] // share
    columns = []
    for k in range(count):
        place = lax.rem(my_x + k, count)
        tile = ints_ref[pl.ds(pl.multiple_of(place * share, share), share)]
        columns.append(jnp.concatenate(
            [tile[:, w].reshape(block, cols).T for w in range(width)], axis=0
        ))
    for q in range(count):
        total = jnp.zeros((width * cols, block), jnp.float32)
        for p in range(count):
            stored = (q, p) in BLOCKS
            piece, place = BLOCKS[(q, p) if stored else (p, q)]
            right = metric_refs[piece][:, place * block:(place + 1) * block]
            total += lax.dot_general(
                columns[p], right, (((1,), (1 if stored else 0,)), ((), ())),
                preferred_element_type=jnp.float32,
            )
        total = total.astype(out_ref.dtype)
        place = lax.rem(my_x + q, count)
        for w in range(width):
            out_ref[w, :, pl.ds(pl.multiple_of(place * block, block), block)] = (
                total[w * cols:(w + 1) * cols]
            )


def fit(metric_parts, me, ints):
    parts, slots, depth, cols = ints.shape
    width = 2
    rows = parts * depth
    return pl.pallas_call(
        fit_kernel,
        out_shape=jax.ShapeDtypeStruct((slots, cols, rows), ints.dtype),
        grid_spec=pltpu.PrefetchScalarGridSpec(
            num_scalar_prefetch=1,
            grid=(slots // width,),
            in_specs=[
                pl.BlockSpec(part.shape, lambda i, me: (0, 0)) for part in metric_parts
            ] + [
                pl.BlockSpec((parts, width, depth, cols), lambda i, me: (0, i, 0, 0)),
            ],
            out_specs=pl.BlockSpec((width, cols, rows), lambda i, me: (i, 0, 0)),
        ),
        compiler_params=pltpu.CompilerParams(vmem_limit_bytes=24 << 20),
        cost_estimate=pl.CostEstimate(
            flops=2 * rows * rows * slots * cols,
            bytes_accessed=2 * rows * rows + 4 * rows * slots * cols,
            transcendentals=0,
        ),
    )(me, *metric_parts, ints)


def close_kernel(fitted_ref, half_ref, out_ref, total_ref):
    step = pl.program_id(0)
    parts, width, depth, cols = half_ref.shape

    @pl.when(step == 0)
    def _():
        total_ref[...] = jnp.zeros_like(total_ref)

    total = total_ref[...]
    for w in range(width):
        right = half_ref[:, w].reshape(parts * depth, cols)
        total += jnp.dot(fitted_ref[w], right, preferred_element_type=jnp.float32)
    total_ref[...] = total

    @pl.when(step == pl.num_programs(0) - 1)
    def _():
        done = total_ref[...].T
        for k in range(out_ref.shape[0]):
            out_ref[k] = done


def close(fitted, half):
    parts, slots, depth, cols = half.shape
    width = 2
    rows = parts * depth
    return pl.pallas_call(
        close_kernel,
        out_shape=jax.ShapeDtypeStruct((X_LEN, cols, cols), jnp.float32),
        grid=(slots // width,),
        in_specs=[
            pl.BlockSpec((width, cols, rows), lambda i: (i, 0, 0)),
            pl.BlockSpec((parts, width, depth, cols), lambda i: (0, i, 0, 0)),
        ],
        out_specs=pl.BlockSpec((X_LEN, cols, cols), lambda i: (0, 0, 0)),
        scratch_shapes=[pltpu.VMEM((cols, cols), jnp.float32)],
        compiler_params=pltpu.CompilerParams(vmem_limit_bytes=24 << 20),
        cost_estimate=pl.CostEstimate(
            flops=2 * rows * slots * cols * cols,
            bytes_accessed=4 * rows * slots * cols,
            transcendentals=0,
        ),
    )(*(pltpu.with_memory_space_constraint(x, pltpu.HBM) for x in (fitted, half)))


def local_density(density, dens_cols, neighbours):
    domain_count = lax.axis_size("dom")
    my_domain = lax.axis_index("dom")
    block_size = density.shape[2]
    neigh_count = neighbours.shape[1]
    my_blocks = lax.dynamic_index_in_dim(neighbours, my_domain, 0, keepdims=False)
    slabs = []
    for offset in range(-RAD, RAD + 1):
        slabs.append(density[0] if offset == 0 else passed_along(density, "dom", -offset)[0])
    row_slabs = jnp.stack(slabs)
    slot_index = (my_blocks - my_domain + RAD) % domain_count
    picked = jnp.take(row_slabs, slot_index, axis=0)
    tile_cols = jnp.take(dens_cols, my_blocks, axis=0)
    matches = (tile_cols[:, None, :] == my_blocks[None, :, None]).astype(jnp.bfloat16)
    tiles = jnp.einsum("jsk,jkab->jasb", matches, picked, preferred_element_type=jnp.float32)
    order = neigh_count * block_size
    return tiles.astype(jnp.bfloat16).reshape(order, order)


def by_slot(array):
    group = lax.axis_size("aux")
    count, slots, cols = array.shape
    return array.transpose(1, 0, 2).reshape(group, slots // group, count, cols)


def exchanged(array):
    return lax.all_to_all(array, "aux", split_axis=0, concat_axis=0, tiled=True)


def body(integrals, density, dens_cols, neighbours, metric):
    ints, rows = integrals[0], metric[0]
    group = lax.axis_size("aux")
    z_len = group // X_LEN
    cols = ints.shape[2]
    me = lax.axis_index("aux")[None]
    line = to_all(metric_copies(rows, me, z_len), "z")
    line = line.reshape(-1, line.shape[2])
    line, ints_out = lax.optimization_barrier((line, by_slot(ints)))
    ints_moved = exchanged(ints_out)
    short = line[:, :2 * rows.shape[1] // X_LEN]
    parts = [line, from_x(line, -1), from_x(short, 2), from_x(short, 1)]
    dense = local_density(density, dens_cols, neighbours)
    half = jnp.einsum("ls,plm->psm", dense, ints, preferred_element_type=jnp.float32)
    half_moved = exchanged(by_slot(half.astype(jnp.bfloat16)))
    fitted = fit(parts, me, ints_moved)
    shares = close(fitted, half_moved)
    shares = jnp.sum(to_all(shares, "x"), axis=0)
    shares = jnp.broadcast_to(shares[None], (z_len, cols, cols))
    return jnp.sum(to_all(shares, "z"), axis=0)[None]


def solution(mesh):
    return jax.shard_map(
        body,
        mesh=mesh,
        in_specs=(
            P("dom", "aux", None, None),
            P("dom", None, None, None),
            P(),
            P(),
            P("dom", "aux", None),
        ),
        out_specs=P("dom", None, None),
        check_vma=False,
    )
```

```python
import jax
import jax.numpy as jnp
from jax import lax
from jax.experimental import pallas as pl
from jax.experimental.pallas import tpu as pltpu
from jax.sharding import PartitionSpec as P


RAD = 2
X_LEN = 4


def passed_along(block, axis, distance):
    devices = range(lax.axis_size(axis))
    route = [((i - distance) % len(devices), i) for i in devices]
    return lax.ppermute(block, axis, route)


def from_x(block, distance):
    count = lax.axis_size("aux")
    z_len = count // X_LEN
    route = [((i - distance * z_len) % count, i) for i in range(count)]
    return lax.ppermute(block, "aux", route)


def groups_along(which):
    z_len = lax.axis_size("aux") // X_LEN
    lines = [[x * z_len + z for z in range(z_len)] for x in range(X_LEN)]
    return lines if which == "z" else [list(line) for line in zip(*lines)]


def to_all(copies, which):
    return lax.all_to_all(
        copies, "aux", split_axis=0, concat_axis=0, tiled=True,
        axis_index_groups=groups_along(which),
    )


def metric_kernel(me_ref, rows_ref, out_ref):
    copies, _, kept = out_ref.shape
    side = rows_ref.shape[1] // X_LEN
    my_x = me_ref[0] // copies
    for k in range(kept // side):
        place = lax.rem(my_x + k, X_LEN)
        block = rows_ref[:, pl.ds(pl.multiple_of(place * side, side), side)]
        for copy in range(copies):
            out_ref[copy, :, k * side:(k + 1) * side] = block


def metric_copies(rows, me, copies):
    count, cols = rows.shape
    return pl.pallas_call(
        metric_kernel,
        out_shape=jax.ShapeDtypeStruct((copies, count, 3 * cols // X_LEN), rows.dtype),
        in_specs=[
            pl.BlockSpec(memory_space=pltpu.SMEM),
            pl.BlockSpec(memory_space=pltpu.VMEM),
        ],
        out_specs=pl.BlockSpec(memory_space=pltpu.VMEM),
        compiler_params=pltpu.CompilerParams(vmem_limit_bytes=4 << 20),
    )(me, rows)


BLOCKS = {
    (0, 0): (0, 0), (0, 1): (0, 1), (0, 2): (0, 2),
    (1, 1): (1, 0), (1, 2): (1, 1), (1, 3): (1, 2),
    (2, 2): (2, 0), (2, 3): (2, 1),
    (3, 3): (3, 0), (3, 0): (3, 1),
}


def fit_kernel(me_ref, *refs):
    *metric_refs, ints_ref, out_ref = refs
    parts, width, depth, cols = ints_ref.shape
    count = len(metric_refs)
    share = parts // count
    block = share * depth
    my_x = me_ref[0] // share
    columns = []
    for k in range(count):
        place = lax.rem(my_x + k, count)
        tile = ints_ref[pl.ds(pl.multiple_of(place * share, share), share)]
        columns.append(jnp.concatenate(
            [tile[:, w].reshape(block, cols).T for w in range(width)], axis=0
        ))
    for q in range(count):
        total = jnp.zeros((width * cols, block), jnp.float32)
        for p in range(count):
            stored = (q, p) in BLOCKS
            piece, place = BLOCKS[(q, p) if stored else (p, q)]
            right = metric_refs[piece][:, place * block:(place + 1) * block]
            total += lax.dot_general(
                columns[p], right, (((1,), (1 if stored else 0,)), ((), ())),
                preferred_element_type=jnp.float32,
            )
        total = total.astype(out_ref.dtype)
        place = lax.rem(my_x + q, count)
        for w in range(width):
            out_ref[w, :, pl.ds(pl.multiple_of(place * block, block), block)] = (
                total[w * cols:(w + 1) * cols]
            )


def fit(metric_parts, me, ints, first, slots):
    parts, _, depth, cols = ints.shape
    width = 2
    rows = parts * depth
    return pl.pallas_call(
        fit_kernel,
        out_shape=jax.ShapeDtypeStruct((slots, cols, rows), ints.dtype),
        grid_spec=pltpu.PrefetchScalarGridSpec(
            num_scalar_prefetch=1,
            grid=(slots // width,),
            in_specs=[
                pl.BlockSpec(part.shape, lambda i, me: (0, 0)) for part in metric_parts
            ] + [
                pl.BlockSpec(
                    (parts, width, depth, cols),
                    lambda i, me: (0, i + first // width, 0, 0),
                ),
            ],
            out_specs=pl.BlockSpec((width, cols, rows), lambda i, me: (i, 0, 0)),
        ),
        compiler_params=pltpu.CompilerParams(vmem_limit_bytes=12 << 20),
        cost_estimate=pl.CostEstimate(
            flops=2 * rows * rows * slots * cols,
            bytes_accessed=2 * rows * rows + 4 * rows * slots * cols,
            transcendentals=0,
        ),
    )(me, *metric_parts, ints)


def close_kernel(*refs):
    *pairs, out_ref, total_ref = refs
    step = pl.program_id(0)

    @pl.when(step == 0)
    def _():
        total_ref[...] = jnp.zeros_like(total_ref)

    total = total_ref[...]
    for fitted_ref, half_ref in zip(pairs[::2], pairs[1::2]):
        parts, width, depth, cols = half_ref.shape
        for w in range(width):
            right = half_ref[:, w].reshape(parts * depth, cols)
            total += jnp.dot(fitted_ref[w], right, preferred_element_type=jnp.float32)
    total_ref[...] = total

    @pl.when(step == pl.num_programs(0) - 1)
    def _():
        done = total_ref[...].T
        for k in range(out_ref.shape[0]):
            out_ref[k] = done


def close(fitted_parts, half, steps):
    parts, slots, depth, cols = half.shape
    rows = parts * depth
    specs, operands, first = [], [], 0
    for fitted in fitted_parts:
        width = fitted.shape[0] // steps
        specs.append(pl.BlockSpec((width, cols, rows), lambda i: (i, 0, 0)))
        specs.append(pl.BlockSpec(
            (parts, width, depth, cols),
            lambda i, start=first // width: (0, i + start, 0, 0),
        ))
        operands += [fitted, half]
        first += fitted.shape[0]
    return pl.pallas_call(
        close_kernel,
        out_shape=jax.ShapeDtypeStruct((X_LEN, cols, cols), jnp.float32),
        grid=(steps,),
        in_specs=specs,
        out_specs=pl.BlockSpec((X_LEN, cols, cols), lambda i: (0, 0, 0)),
        scratch_shapes=[pltpu.VMEM((cols, cols), jnp.float32)],
        compiler_params=pltpu.CompilerParams(vmem_limit_bytes=12 << 20),
        cost_estimate=pl.CostEstimate(
            flops=2 * rows * slots * cols * cols,
            bytes_accessed=4 * rows * slots * cols,
            transcendentals=0,
        ),
    )(*operands)


def local_density(density, dens_cols, neighbours):
    domain_count = lax.axis_size("dom")
    my_domain = lax.axis_index("dom")
    block_size = density.shape[2]
    neigh_count = neighbours.shape[1]
    my_blocks = lax.dynamic_index_in_dim(neighbours, my_domain, 0, keepdims=False)
    slabs = []
    for offset in range(-RAD, RAD + 1):
        slabs.append(density[0] if offset == 0 else passed_along(density, "dom", -offset)[0])
    row_slabs = jnp.stack(slabs)
    slot_index = (my_blocks - my_domain + RAD) % domain_count
    picked = jnp.take(row_slabs, slot_index, axis=0)
    tile_cols = jnp.take(dens_cols, my_blocks, axis=0)
    matches = (tile_cols[:, None, :] == my_blocks[None, :, None]).astype(jnp.bfloat16)
    tiles = jnp.einsum("jsk,jkab->jasb", matches, picked, preferred_element_type=jnp.float32)
    order = neigh_count * block_size
    return tiles.astype(jnp.bfloat16).reshape(order, order)


def by_slot(array):
    group = lax.axis_size("aux")
    count, slots, cols = array.shape
    return array.transpose(1, 0, 2).reshape(group, slots // group, count, cols)


def exchanged(array):
    return lax.all_to_all(array, "aux", split_axis=0, concat_axis=0, tiled=True)


def body(integrals, density, dens_cols, neighbours, metric):
    ints, rows = integrals[0], metric[0]
    group = lax.axis_size("aux")
    z_len = group // X_LEN
    cols = ints.shape[2]
    me = lax.axis_index("aux")[None]
    line = to_all(metric_copies(rows, me, z_len), "z")
    line = line.reshape(-1, line.shape[2])
    line, ints_out = lax.optimization_barrier((line, by_slot(ints)))
    ints_moved = exchanged(ints_out)
    short = line[:, :2 * rows.shape[1] // X_LEN]
    parts = [line, from_x(line, -1), from_x(short, 2), from_x(short, 1)]
    dense = local_density(density, dens_cols, neighbours)
    half = jnp.einsum("ls,plm->psm", dense, ints, preferred_element_type=jnp.float32)
    half_moved = exchanged(by_slot(half.astype(jnp.bfloat16)))
    most = 3 * ints_moved.shape[1] // 4
    rest = fit(parts, me, ints_moved, most, ints_moved.shape[1] - most)
    fitted = [
        fit(parts, me, ints_moved, 0, most),
        pltpu.with_memory_space_constraint(rest, pltpu.HBM),
    ]
    shares = close(fitted, half_moved, 4)
    shares = jnp.sum(to_all(shares, "x"), axis=0).astype(jnp.bfloat16)
    shares = jnp.broadcast_to(shares[None], (z_len, cols, cols))
    shares = to_all(shares, "z").astype(jnp.float32)
    return jnp.sum(shares, axis=0)[None]


def solution(mesh):
    return jax.shard_map(
        body,
        mesh=mesh,
        in_specs=(
            P("dom", "aux", None, None),
            P("dom", None, None, None),
            P(),
            P(),
            P("dom", "aux", None),
        ),
        out_specs=P("dom", None, None),
        check_vma=False,
    )
```

```python
import jax
import jax.numpy as jnp
from jax import lax
from jax.experimental import pallas as pl
from jax.experimental.pallas import tpu as pltpu
from jax.sharding import PartitionSpec as P


RAD = 2
X_LEN = 4


def passed_along(block, axis, distance):
    devices = range(lax.axis_size(axis))
    route = [((i - distance) % len(devices), i) for i in devices]
    return lax.ppermute(block, axis, route)


def from_x(block, distance):
    count = lax.axis_size("aux")
    z_len = count // X_LEN
    route = [((i - distance * z_len) % count, i) for i in range(count)]
    return lax.ppermute(block, "aux", route)


def groups_along(which):
    z_len = lax.axis_size("aux") // X_LEN
    lines = [[x * z_len + z for z in range(z_len)] for x in range(X_LEN)]
    return lines if which == "z" else [list(line) for line in zip(*lines)]


def to_all(copies, which):
    return lax.all_to_all(
        copies, "aux", split_axis=0, concat_axis=0, tiled=True,
        axis_index_groups=groups_along(which),
    )


def metric_kernel(me_ref, rows_ref, out_ref):
    copies, _, kept = out_ref.shape
    side = rows_ref.shape[1] // X_LEN
    my_x = me_ref[0] // copies
    for k in range(kept // side):
        place = lax.rem(my_x + k, X_LEN)
        block = rows_ref[:, pl.ds(pl.multiple_of(place * side, side), side)]
        for copy in range(copies):
            out_ref[copy, :, k * side:(k + 1) * side] = block


def metric_copies(rows, me, copies):
    count, cols = rows.shape
    return pl.pallas_call(
        metric_kernel,
        out_shape=jax.ShapeDtypeStruct((copies, count, 3 * cols // X_LEN), rows.dtype),
        in_specs=[
            pl.BlockSpec(memory_space=pltpu.SMEM),
            pl.BlockSpec(memory_space=pltpu.VMEM),
        ],
        out_specs=pl.BlockSpec(memory_space=pltpu.VMEM),
        compiler_params=pltpu.CompilerParams(vmem_limit_bytes=4 << 20),
    )(me, rows)


BLOCKS = {
    (0, 0): (0, 0), (0, 1): (0, 1), (0, 2): (0, 2),
    (1, 1): (1, 0), (1, 2): (1, 1), (1, 3): (1, 2),
    (2, 2): (2, 0), (2, 3): (2, 1),
    (3, 3): (3, 0), (3, 0): (3, 1),
}


def fit_kernel(me_ref, *refs):
    *metric_refs, ints_ref, out_ref = refs
    parts, width, depth, cols = ints_ref.shape
    count = len(metric_refs)
    share = parts // count
    block = share * depth
    my_x, my_z = me_ref[0] // share, lax.rem(me_ref[0], share)
    columns = []
    for k in range(count):
        place = lax.rem(my_x + k, count)
        tile = ints_ref[pl.ds(pl.multiple_of(place * share, share), share)]
        columns.append(jnp.concatenate(
            [tile[:, w].reshape(block, cols).T for w in range(width)], axis=0
        ))
    for q in range(count):
        total = jnp.zeros((width * cols, block), jnp.float32)
        for p in range(count):
            stored = (q, p) in BLOCKS
            piece, place = BLOCKS[(q, p) if stored else (p, q)]
            right = metric_refs[piece][:, place * block:(place + 1) * block]
            total += lax.dot_general(
                columns[p], right, (((1,), (1 if stored else 0,)), ((), ())),
                preferred_element_type=jnp.float32,
            )
        total = pltpu.roll(total, lax.rem(block - depth * my_z, block), 1).astype(out_ref.dtype)
        for w in range(width):
            out_ref[w, :, q * block:(q + 1) * block] = total[w * cols:(w + 1) * cols]


def fit(metric_parts, me, ints):
    parts, slots, depth, cols = ints.shape
    width = 2
    rows = parts * depth
    return pl.pallas_call(
        fit_kernel,
        out_shape=jax.ShapeDtypeStruct((slots, cols, rows), ints.dtype),
        grid_spec=pltpu.PrefetchScalarGridSpec(
            num_scalar_prefetch=1,
            grid=(slots // width,),
            in_specs=[
                pl.BlockSpec(part.shape, lambda i, me: (0, 0)) for part in metric_parts
            ] + [
                pl.BlockSpec((parts, width, depth, cols), lambda i, me: (0, i, 0, 0)),
            ],
            out_specs=pl.BlockSpec((width, cols, rows), lambda i, me: (i, 0, 0)),
        ),
        compiler_params=pltpu.CompilerParams(vmem_limit_bytes=12 << 20),
        cost_estimate=pl.CostEstimate(
            flops=2 * rows * rows * slots * cols,
            bytes_accessed=2 * rows * rows + 4 * rows * slots * cols,
            transcendentals=0,
        ),
    )(me, *metric_parts, ints)


def spread_kernel(me_ref, half_ref, *out_refs):
    group, slots = len(out_refs), out_refs[0].shape[0]
    z_len = group // X_LEN
    my_x, my_z = me_ref[0] // z_len, lax.rem(me_ref[0], z_len)
    for k, out_ref in enumerate(out_refs):
        dx, dz = k // z_len, k % z_len
        owner_x = lax.rem(my_x + X_LEN - dx, X_LEN)
        owner = owner_x * z_len + lax.rem(my_z + z_len - dz, z_len)
        tile = half_ref[:, pl.ds(pl.multiple_of(owner * slots, slots), slots), :]
        out_ref[...] = jnp.swapaxes(tile, 0, 1)


def spread(half, me):
    group = lax.axis_size("aux")
    count, slots, cols = half.shape
    piece = jax.ShapeDtypeStruct((slots // group, count, cols), half.dtype)
    return pl.pallas_call(
        spread_kernel,
        out_shape=[piece] * group,
        in_specs=[
            pl.BlockSpec(memory_space=pltpu.SMEM),
            pl.BlockSpec(memory_space=pltpu.VMEM),
        ],
        out_specs=[pl.BlockSpec(memory_space=pltpu.VMEM)] * group,
        compiler_params=pltpu.CompilerParams(vmem_limit_bytes=16 << 20),
        cost_estimate=pl.CostEstimate(
            flops=0, bytes_accessed=4 * half.size, transcendentals=0,
        ),
    )(me, half)


def moved(pieces):
    z_len = len(pieces) // X_LEN
    grid = [(x, z) for x in range(X_LEN) for z in range(z_len)]
    out = list(pieces)
    for dz in sorted(range(z_len), key=lambda dz: (-min(dz, z_len - dz), dz)):
        for dx in range(X_LEN):
            k = dx * z_len + dz
            if k:
                route = [
                    ((x + dx) % X_LEN * z_len + (z + dz) % z_len, x * z_len + z)
                    for x, z in grid
                ]
                out[k] = lax.ppermute(pieces[k], "aux", route)
    return out


def close_kernel(fitted_ref, *refs):
    *half_refs, out_ref, total_ref = refs
    step = pl.program_id(0)
    width, cols, _ = fitted_ref.shape

    @pl.when(step == 0)
    def _():
        total_ref[...] = jnp.zeros_like(total_ref)

    total = total_ref[...]
    for w in range(0, width, 2):
        left = jnp.concatenate([fitted_ref[w], fitted_ref[w + 1]], axis=0)
        right = jnp.concatenate([
            jnp.concatenate([ref[v] for ref in half_refs], axis=0) for v in (w, w + 1)
        ], axis=1)
        pair = jnp.dot(left, right, preferred_element_type=jnp.float32)
        total += pair[:cols, :cols] + pair[cols:, cols:]
    total_ref[...] = total

    @pl.when(step == pl.num_programs(0) - 1)
    def _():
        done = total_ref[...].T
        for k in range(out_ref.shape[0]):
            out_ref[k] = done


def close(fitted, pieces):
    slots, depth, cols = pieces[0].shape
    rows = fitted.shape[2]
    width = 4
    return pl.pallas_call(
        close_kernel,
        out_shape=jax.ShapeDtypeStruct((X_LEN, cols, cols), jnp.float32),
        grid=(slots // width,),
        in_specs=[pl.BlockSpec((width, cols, rows), lambda i: (i, 0, 0))] + [
            pl.BlockSpec((width, depth, cols), lambda i: (i, 0, 0)) for _ in pieces
        ],
        out_specs=pl.BlockSpec((X_LEN, cols, cols), lambda i: (0, 0, 0)),
        scratch_shapes=[pltpu.VMEM((cols, cols), jnp.float32)],
        compiler_params=pltpu.CompilerParams(vmem_limit_bytes=12 << 20),
        cost_estimate=pl.CostEstimate(
            flops=2 * rows * slots * cols * cols,
            bytes_accessed=4 * rows * slots * cols,
            transcendentals=0,
        ),
    )(fitted, *pieces)


def local_density(density, dens_cols, neighbours):
    domain_count = lax.axis_size("dom")
    my_domain = lax.axis_index("dom")
    block_size = density.shape[2]
    neigh_count = neighbours.shape[1]
    my_blocks = lax.dynamic_index_in_dim(neighbours, my_domain, 0, keepdims=False)
    slabs = []
    for offset in range(-RAD, RAD + 1):
        slabs.append(density[0] if offset == 0 else passed_along(density, "dom", -offset)[0])
    row_slabs = jnp.stack(slabs)
    slot_index = (my_blocks - my_domain + RAD) % domain_count
    picked = jnp.take(row_slabs, slot_index, axis=0)
    tile_cols = jnp.take(dens_cols, my_blocks, axis=0)
    matches = (tile_cols[:, None, :] == my_blocks[None, :, None]).astype(jnp.bfloat16)
    tiles = jnp.einsum("jsk,jkab->jasb", matches, picked, preferred_element_type=jnp.float32)
    order = neigh_count * block_size
    return tiles.astype(jnp.bfloat16).reshape(order, order)


def by_slot(array):
    group = lax.axis_size("aux")
    count, slots, cols = array.shape
    return array.transpose(1, 0, 2).reshape(group, slots // group, count, cols)


def exchanged(array):
    return lax.all_to_all(array, "aux", split_axis=0, concat_axis=0, tiled=True)


def body(integrals, density, dens_cols, neighbours, metric):
    ints, rows = integrals[0], metric[0]
    group = lax.axis_size("aux")
    z_len = group // X_LEN
    cols = ints.shape[2]
    me = lax.axis_index("aux")[None]
    line = to_all(metric_copies(rows, me, z_len), "z")
    line = line.reshape(-1, line.shape[2])
    line, ints_out = lax.optimization_barrier((line, by_slot(ints)))
    ints_moved = exchanged(ints_out)
    short = line[:, :2 * rows.shape[1] // X_LEN]
    parts = [line, from_x(line, -1), from_x(short, 2), from_x(short, 1)]
    dense = local_density(density, dens_cols, neighbours)
    half = jnp.einsum("ls,plm->psm", dense, ints, preferred_element_type=jnp.float32)
    pieces = spread(half.astype(jnp.bfloat16), me)
    pieces = moved(pieces)
    first = jnp.sum(jnp.arange(1, lax.axis_size("aux")) <= me[0], dtype=jnp.int32)[None]
    fitted = fit(parts, first, ints_moved)
    shares = close(fitted, pieces)
    shares = jnp.sum(to_all(shares, "x"), axis=0).astype(jnp.bfloat16)
    shares = jnp.broadcast_to(shares[None], (z_len, cols, cols))
    shares = to_all(shares, "z").astype(jnp.float32)
    return jnp.sum(shares, axis=0)[None]


def solution(mesh):
    return jax.shard_map(
        body,
        mesh=mesh,
        in_specs=(
            P("dom", "aux", None, None),
            P("dom", None, None, None),
            P(),
            P(),
            P("dom", "aux", None),
        ),
        out_specs=P("dom", None, None),
        check_vma=False,
    )
```

```python
import jax
import jax.numpy as jnp
from jax import lax
from jax.experimental import pallas as pl
from jax.experimental.pallas import tpu as pltpu
from jax.sharding import PartitionSpec as P


RAD = 2
X_LEN, Z_LEN = 4, 8


def passed_along(block, axis, distance):
    devices = range(lax.axis_size(axis))
    route = [((i - distance) % len(devices), i) for i in devices]
    return lax.ppermute(block, axis, route)


def from_grid(block, dx, dz):
    route = []
    for x in range(X_LEN):
        for z in range(Z_LEN):
            source = (x - dx) % X_LEN * Z_LEN + (z - dz) % Z_LEN
            route.append((source, x * Z_LEN + z))
    return lax.ppermute(block, "aux", route)


def groups_along(which):
    lines = [[x * Z_LEN + z for z in range(Z_LEN)] for x in range(X_LEN)]
    return lines if which == "z" else [list(line) for line in zip(*lines)]


def to_all(copies, which):
    return lax.all_to_all(
        copies, "aux", split_axis=0, concat_axis=0, tiled=True,
        axis_index_groups=groups_along(which),
    )


def metric_kernel(me_ref, rows_ref, out_ref):
    kept = out_ref.shape[1]
    side = rows_ref.shape[1] // X_LEN
    my_x = me_ref[0] // Z_LEN
    for k in range(kept // side):
        place = lax.rem(my_x + k, X_LEN)
        out_ref[:, k * side:(k + 1) * side] = (
            rows_ref[:, pl.ds(pl.multiple_of(place * side, side), side)]
        )


def line_kernel(me_ref, *refs):
    *piece_refs, line_ref, short_ref = refs
    count = piece_refs[0].shape[0]
    my_z = lax.rem(me_ref[0], Z_LEN)
    for k, piece_ref in enumerate(piece_refs):
        place = lax.rem(my_z + (Z_LEN - k), Z_LEN)
        rows = pl.ds(pl.multiple_of(place * count, count), count)
        line_ref[rows, :] = piece_ref[...]
        short_ref[rows, :] = piece_ref[:, :short_ref.shape[1]]


def in_vmem(kernel, shapes, me, *arrays):
    whole = pl.BlockSpec(memory_space=pltpu.VMEM)
    return pl.pallas_call(
        kernel,
        out_shape=[jax.ShapeDtypeStruct(shape, arrays[0].dtype) for shape in shapes],
        in_specs=[pl.BlockSpec(memory_space=pltpu.SMEM)] + [whole] * len(arrays),
        out_specs=[whole] * len(shapes),
        compiler_params=pltpu.CompilerParams(vmem_limit_bytes=4 << 20),
    )(me, *arrays)


BLOCKS = {
    (0, 0): (0, 0), (0, 1): (0, 1), (0, 2): (0, 2),
    (1, 1): (1, 0), (1, 2): (1, 1), (1, 3): (1, 2),
    (2, 2): (2, 0), (2, 3): (2, 1),
    (3, 3): (3, 0), (3, 0): (3, 1),
}


def fit_kernel(me_ref, *refs):
    *metric_refs, ints_ref, out_ref = refs
    parts, width, depth, cols = ints_ref.shape
    count = len(metric_refs)
    share = parts // count
    block = share * depth
    my_x = me_ref[0] // share
    columns = []
    for k in range(count):
        place = lax.rem(my_x + k, count)
        tile = ints_ref[pl.ds(pl.multiple_of(place * share, share), share)]
        columns.append(jnp.concatenate(
            [tile[:, w].reshape(block, cols).T for w in range(width)], axis=0
        ))
    for q in range(count):
        total = jnp.zeros((width * cols, block), jnp.float32)
        for p in range(count):
            stored = (q, p) in BLOCKS
            piece, place = BLOCKS[(q, p) if stored else (p, q)]
            right = metric_refs[piece][:, place * block:(place + 1) * block]
            total += lax.dot_general(
                columns[p], right, (((1,), (1 if stored else 0,)), ((), ())),
                preferred_element_type=jnp.float32,
            )
        total = total.astype(out_ref.dtype)
        place = lax.rem(my_x + q, count)
        for w in range(width):
            out_ref[w, :, pl.ds(pl.multiple_of(place * block, block), block)] = (
                total[w * cols:(w + 1) * cols]
            )


def fit(metric_parts, me, ints, first, slots):
    parts, _, depth, cols = ints.shape
    width = 2
    rows = parts * depth
    return pl.pallas_call(
        fit_kernel,
        out_shape=jax.ShapeDtypeStruct((slots, cols, rows), ints.dtype),
        grid_spec=pltpu.PrefetchScalarGridSpec(
            num_scalar_prefetch=1,
            grid=(slots // width,),
            in_specs=[
                pl.BlockSpec(part.shape, lambda i, me: (0, 0)) for part in metric_parts
            ] + [
                pl.BlockSpec(
                    (parts, width, depth, cols),
                    lambda i, me: (0, i + first // width, 0, 0),
                ),
            ],
            out_specs=pl.BlockSpec((width, cols, rows), lambda i, me: (i, 0, 0)),
        ),
        compiler_params=pltpu.CompilerParams(vmem_limit_bytes=12 << 20),
        cost_estimate=pl.CostEstimate(
            flops=2 * rows * rows * slots * cols,
            bytes_accessed=2 * rows * rows + 4 * rows * slots * cols,
            transcendentals=0,
        ),
    )(me, *metric_parts, ints)


def close_kernel(*refs):
    *pairs, out_ref, total_ref = refs
    step = pl.program_id(0)

    @pl.when(step == 0)
    def _():
        total_ref[...] = jnp.zeros_like(total_ref)

    lefts, rights = [], []
    for fitted_ref, half_ref in zip(pairs[::2], pairs[1::2]):
        parts, width, depth, cols = half_ref.shape
        for w in range(width):
            lefts.append(fitted_ref[w])
            rights.append(half_ref[:, w].reshape(parts * depth, cols))
    total = total_ref[...]
    for k in range(0, len(lefts), 2):
        both = jnp.dot(
            jnp.concatenate(lefts[k:k + 2], axis=0),
            jnp.concatenate(rights[k:k + 2], axis=1),
            preferred_element_type=jnp.float32,
        )
        total += both[:cols, :cols] + both[cols:, cols:]
    total_ref[...] = total

    @pl.when(step == pl.num_programs(0) - 1)
    def _():
        done = total_ref[...].T
        for k in range(out_ref.shape[0]):
            out_ref[k] = done


def close(fitted_parts, half, steps):
    parts, slots, depth, cols = half.shape
    rows = parts * depth
    specs, operands, first = [], [], 0
    for fitted in fitted_parts:
        width = fitted.shape[0] // steps
        specs.append(pl.BlockSpec((width, cols, rows), lambda i: (i, 0, 0)))
        specs.append(pl.BlockSpec(
            (parts, width, depth, cols),
            lambda i, start=first // width: (0, i + start, 0, 0),
        ))
        operands += [fitted, half]
        first += fitted.shape[0]
    return pl.pallas_call(
        close_kernel,
        out_shape=jax.ShapeDtypeStruct((X_LEN, cols, cols), jnp.float32),
        grid=(steps,),
        in_specs=specs,
        out_specs=pl.BlockSpec((X_LEN, cols, cols), lambda i: (0, 0, 0)),
        scratch_shapes=[pltpu.VMEM((cols, cols), jnp.float32)],
        compiler_params=pltpu.CompilerParams(vmem_limit_bytes=12 << 20),
        cost_estimate=pl.CostEstimate(
            flops=2 * rows * slots * cols * cols,
            bytes_accessed=4 * rows * slots * cols,
            transcendentals=0,
        ),
    )(*operands)


def local_density(density, dens_cols, neighbours):
    domain_count = lax.axis_size("dom")
    my_domain = lax.axis_index("dom")
    block_size = density.shape[2]
    neigh_count = neighbours.shape[1]
    my_blocks = lax.dynamic_index_in_dim(neighbours, my_domain, 0, keepdims=False)
    slabs = []
    for offset in range(-RAD, RAD + 1):
        slabs.append(density[0] if offset == 0 else passed_along(density, "dom", -offset)[0])
    row_slabs = jnp.stack(slabs)
    slot_index = (my_blocks - my_domain + RAD) % domain_count
    picked = jnp.take(row_slabs, slot_index, axis=0)
    tile_cols = jnp.take(dens_cols, my_blocks, axis=0)
    matches = (tile_cols[:, None, :] == my_blocks[None, :, None]).astype(jnp.bfloat16)
    tiles = jnp.einsum("jsk,jkab->jasb", matches, picked, preferred_element_type=jnp.float32)
    order = neigh_count * block_size
    return tiles.astype(jnp.bfloat16).reshape(order, order)


def by_slot(array):
    group = lax.axis_size("aux")
    count, slots, cols = array.shape
    return array.transpose(1, 0, 2).reshape(group, slots // group, count, cols)


def exchanged(array):
    return lax.all_to_all(array, "aux", split_axis=0, concat_axis=0, tiled=True)


def body(integrals, density, dens_cols, neighbours, metric):
    ints, rows = integrals[0], metric[0]
    cols = ints.shape[2]
    count, side = rows.shape[0], rows.shape[1] // X_LEN
    me = lax.axis_index("aux")[None]
    ints_moved = exchanged(by_slot(ints))
    kept, = in_vmem(metric_kernel, [(count, 3 * side)], me, rows)
    pieces = [kept] + [from_grid(kept, 0, k) for k in range(1, Z_LEN)]
    dense = local_density(density, dens_cols, neighbours)
    half = jnp.einsum("ls,plm->psm", dense, ints, preferred_element_type=jnp.float32)
    half_moved = exchanged(by_slot(half.astype(jnp.bfloat16)))
    shapes = [(Z_LEN * count, 3 * side), (Z_LEN * count, 2 * side)]
    line, short = in_vmem(line_kernel, shapes, me, *pieces)
    parts = [line, from_grid(line, -1, 0), from_grid(short, 2, 0), from_grid(short, 1, 0)]
    most = 3 * ints_moved.shape[1] // 4
    rest = fit(parts, me, ints_moved, most, ints_moved.shape[1] - most)
    fitted = [
        fit(parts, me, ints_moved, 0, most),
        pltpu.with_memory_space_constraint(rest, pltpu.HBM),
    ]
    shares = close(fitted, half_moved, 4)
    shares = jnp.sum(to_all(shares, "x"), axis=0).astype(jnp.bfloat16)
    shares = jnp.broadcast_to(shares[None], (Z_LEN, cols, cols))
    shares = to_all(shares, "z").astype(jnp.float32)
    return jnp.sum(shares, axis=0)[None]


def solution(mesh):
    return jax.shard_map(
        body,
        mesh=mesh,
        in_specs=(
            P("dom", "aux", None, None),
            P("dom", None, None, None),
            P(),
            P(),
            P("dom", "aux", None),
        ),
        out_specs=P("dom", None, None),
        check_vma=False,
    )
```

```python
import jax
import jax.numpy as jnp
from jax import lax
from jax.experimental import pallas as pl
from jax.experimental.pallas import tpu as pltpu
from jax.sharding import PartitionSpec as P


RAD = 2
X_LEN, Z_LEN = 4, 8


def passed_along(block, axis, distance):
    devices = range(lax.axis_size(axis))
    route = [((i - distance) % len(devices), i) for i in devices]
    return lax.ppermute(block, axis, route)


def from_grid(block, dx, dz):
    route = []
    for x in range(X_LEN):
        for z in range(Z_LEN):
            source = (x - dx) % X_LEN * Z_LEN + (z - dz) % Z_LEN
            route.append((source, x * Z_LEN + z))
    return lax.ppermute(block, "aux", route)


def groups_along(which):
    lines = [[x * Z_LEN + z for z in range(Z_LEN)] for x in range(X_LEN)]
    return lines if which == "z" else [list(line) for line in zip(*lines)]


def to_all(copies, which):
    return lax.all_to_all(
        copies, "aux", split_axis=0, concat_axis=0, tiled=True,
        axis_index_groups=groups_along(which),
    )


def metric_kernel(me_ref, rows_ref, out_ref):
    kept = out_ref.shape[1]
    side = rows_ref.shape[1] // X_LEN
    my_x = me_ref[0] // Z_LEN
    for k in range(kept // side):
        place = lax.rem(my_x + k, X_LEN)
        out_ref[:, k * side:(k + 1) * side] = (
            rows_ref[:, pl.ds(pl.multiple_of(place * side, side), side)]
        )


def line_kernel(me_ref, *refs):
    *piece_refs, line_ref, short_ref = refs
    count = piece_refs[0].shape[0]
    my_z = lax.rem(me_ref[0], Z_LEN)
    for k, piece_ref in enumerate(piece_refs):
        place = lax.rem(my_z + (Z_LEN - k), Z_LEN)
        rows = pl.ds(pl.multiple_of(place * count, count), count)
        line_ref[rows, :] = piece_ref[...]
        short_ref[rows, :] = piece_ref[:, :short_ref.shape[1]]


def in_vmem(kernel, shapes, me, *arrays):
    whole = pl.BlockSpec(memory_space=pltpu.VMEM)
    return pl.pallas_call(
        kernel,
        out_shape=[jax.ShapeDtypeStruct(shape, arrays[0].dtype) for shape in shapes],
        in_specs=[pl.BlockSpec(memory_space=pltpu.SMEM)] + [whole] * len(arrays),
        out_specs=[whole] * len(shapes),
        compiler_params=pltpu.CompilerParams(vmem_limit_bytes=4 << 20),
    )(me, *arrays)


BLOCKS = {
    (0, 0): (0, 0), (0, 1): (0, 1), (0, 2): (0, 2),
    (1, 1): (1, 0), (1, 2): (1, 1), (1, 3): (1, 2),
    (2, 2): (2, 0), (2, 3): (2, 1),
    (3, 3): (3, 0), (3, 0): (3, 1),
}


def fit_kernel(me_ref, *refs):
    *metric_refs, ints_ref, out_ref = refs
    parts, width, depth, cols = ints_ref.shape
    count = len(metric_refs)
    share = parts // count
    block = share * depth
    my_x = me_ref[0] // share
    columns = []
    for k in range(count):
        place = lax.rem(my_x + k, count)
        tile = ints_ref[pl.ds(pl.multiple_of(place * share, share), share)]
        columns.append(jnp.concatenate(
            [tile[:, w].reshape(block, cols).T for w in range(width)], axis=0
        ))
    for q in range(count):
        total = jnp.zeros((width * cols, block), jnp.float32)
        for p in range(count):
            stored = (q, p) in BLOCKS
            piece, place = BLOCKS[(q, p) if stored else (p, q)]
            right = metric_refs[piece][:, place * block:(place + 1) * block]
            total += lax.dot_general(
                columns[p], right, (((1,), (1 if stored else 0,)), ((), ())),
                preferred_element_type=jnp.float32,
            )
        total = total.astype(out_ref.dtype)
        place = lax.rem(my_x + q, count)
        for w in range(width):
            out_ref[w, :, pl.ds(pl.multiple_of(place * block, block), block)] = (
                total[w * cols:(w + 1) * cols]
            )


def fit(metric_parts, me, ints, first, slots):
    parts, _, depth, cols = ints.shape
    width = 2
    rows = parts * depth
    return pl.pallas_call(
        fit_kernel,
        out_shape=jax.ShapeDtypeStruct((slots, cols, rows), ints.dtype),
        grid_spec=pltpu.PrefetchScalarGridSpec(
            num_scalar_prefetch=1,
            grid=(slots // width,),
            in_specs=[
                pl.BlockSpec(part.shape, lambda i, me: (0, 0)) for part in metric_parts
            ] + [
                pl.BlockSpec(
                    (parts, width, depth, cols),
                    lambda i, me: (0, i + first // width, 0, 0),
                ),
            ],
            out_specs=pl.BlockSpec((width, cols, rows), lambda i, me: (i, 0, 0)),
        ),
        compiler_params=pltpu.CompilerParams(vmem_limit_bytes=12 << 20),
        cost_estimate=pl.CostEstimate(
            flops=2 * rows * rows * slots * cols,
            bytes_accessed=2 * rows * rows + 4 * rows * slots * cols,
            transcendentals=0,
        ),
    )(me, *metric_parts, ints)


def close_kernel(most_ref, rest_ref, half_ref, out_ref, half_buf, rest_buf, sems):
    chunks, parts, width, depth, cols = half_buf.shape
    copies = [
        pltpu.make_async_copy(
            half_ref.at[:, pl.ds(width * c, width)], half_buf.at[c], sems.at[c],
        )
        for c in range(chunks)
    ]
    copies.append(pltpu.make_async_copy(rest_ref, rest_buf, sems.at[chunks]))
    for copy in copies:
        copy.start()
    total = jnp.zeros((cols, cols), jnp.float32)
    for c in range(chunks):
        copies[c].wait()
        if c == chunks - 1:
            copies[chunks].wait()
        for w in range(0, width, 2):
            slots = (w, w + 1)
            if c < chunks - 1:
                lefts = [most_ref[width * c + v] for v in slots]
            else:
                lefts = [rest_buf[v] for v in slots]
            rights = [half_buf[c, :, v].reshape(parts * depth, cols) for v in slots]
            both = jnp.dot(
                jnp.concatenate(lefts, axis=0), jnp.concatenate(rights, axis=1),
                preferred_element_type=jnp.float32,
            )
            total += both[:cols, :cols] + both[cols:, cols:]
    done = total.T
    for k in range(out_ref.shape[0]):
        out_ref[k] = done


def close(most, rest, half):
    parts, slots, depth, cols = half.shape
    width = rest.shape[0]
    chunks = slots // width
    vmem, hbm = pltpu.VMEM, pltpu.HBM
    return pl.pallas_call(
        close_kernel,
        out_shape=jax.ShapeDtypeStruct((X_LEN, cols, cols), jnp.float32),
        in_specs=[pl.BlockSpec(memory_space=space) for space in (vmem, hbm, hbm)],
        out_specs=pl.BlockSpec(memory_space=vmem),
        scratch_shapes=[
            pltpu.VMEM((chunks, parts, width, depth, cols), half.dtype),
            pltpu.VMEM(rest.shape, rest.dtype),
            pltpu.SemaphoreType.DMA((chunks + 1,)),
        ],
        compiler_params=pltpu.CompilerParams(vmem_limit_bytes=16 << 20),
        cost_estimate=pl.CostEstimate(
            flops=2 * parts * depth * slots * cols * cols,
            bytes_accessed=4 * parts * depth * slots * cols,
            transcendentals=0,
        ),
    )(most, *(pltpu.with_memory_space_constraint(x, hbm) for x in (rest, half)))


def swap_kernel(in_ref, out_ref):
    out_ref[...] = jnp.swapaxes(in_ref[...], 0, 1)


def slot_major(array, width):
    count, slots, cols = array.shape
    return pl.pallas_call(
        swap_kernel,
        out_shape=pltpu.HBM((slots, count, cols), array.dtype),
        grid=(slots // width,),
        in_specs=[pl.BlockSpec((count, width, cols), lambda i: (0, i, 0))],
        out_specs=pl.BlockSpec((width, count, cols), lambda i: (i, 0, 0)),
        compiler_params=pltpu.CompilerParams(vmem_limit_bytes=8 << 20),
        cost_estimate=pl.CostEstimate(
            flops=0, bytes_accessed=4 * array.size, transcendentals=0,
        ),
    )(pltpu.with_memory_space_constraint(array, pltpu.HBM))


def local_density(density, dens_cols, neighbours):
    domain_count = lax.axis_size("dom")
    my_domain = lax.axis_index("dom")
    block_size = density.shape[2]
    neigh_count = neighbours.shape[1]
    my_blocks = lax.dynamic_index_in_dim(neighbours, my_domain, 0, keepdims=False)
    slabs = []
    for offset in range(-RAD, RAD + 1):
        slabs.append(density[0] if offset == 0 else passed_along(density, "dom", -offset)[0])
    row_slabs = jnp.stack(slabs)
    slot_index = (my_blocks - my_domain + RAD) % domain_count
    picked = jnp.take(row_slabs, slot_index, axis=0)
    tile_cols = jnp.take(dens_cols, my_blocks, axis=0)
    matches = (tile_cols[:, None, :] == my_blocks[None, :, None]).astype(jnp.bfloat16)
    tiles = jnp.einsum("jsk,jkab->jasb", matches, picked, preferred_element_type=jnp.float32)
    order = neigh_count * block_size
    return tiles.astype(jnp.bfloat16).reshape(order, order)


def by_slot(array):
    group = lax.axis_size("aux")
    count, slots, cols = array.shape
    return array.transpose(1, 0, 2).reshape(group, slots // group, count, cols)


def exchanged(array):
    return lax.all_to_all(array, "aux", split_axis=0, concat_axis=0, tiled=True)


def body(integrals, density, dens_cols, neighbours, metric):
    ints, rows = integrals[0], metric[0]
    cols = ints.shape[2]
    count, side = rows.shape[0], rows.shape[1] // X_LEN
    me = lax.axis_index("aux")[None]
    ints_out = slot_major(ints, 64)
    group = lax.axis_size("aux")
    ints_moved = exchanged(ints_out.reshape(group, -1, count, cols))
    kept, = in_vmem(metric_kernel, [(count, 3 * side)], me, rows)
    pieces = [kept] + [from_grid(kept, 0, k) for k in range(1, Z_LEN)]
    dense = local_density(density, dens_cols, neighbours)
    half = jnp.einsum("ls,plm->psm", dense, ints, preferred_element_type=jnp.float32)
    half_moved = exchanged(by_slot(half.astype(jnp.bfloat16)))
    shapes = [(Z_LEN * count, 3 * side), (Z_LEN * count, 2 * side)]
    line, short = in_vmem(line_kernel, shapes, me, *pieces)
    parts = [line, from_grid(line, -1, 0), from_grid(short, 2, 0), from_grid(short, 1, 0)]
    most = 3 * ints_moved.shape[1] // 4
    rest = fit(parts, me, ints_moved, most, ints_moved.shape[1] - most)
    shares = close(fit(parts, me, ints_moved, 0, most), rest, half_moved)
    shares = jnp.sum(to_all(shares, "x"), axis=0).astype(jnp.bfloat16)
    shares = jnp.broadcast_to(shares[None], (Z_LEN, cols, cols))
    shares = to_all(shares, "z").astype(jnp.float32)
    return jnp.sum(shares, axis=0)[None]


def solution(mesh):
    return jax.shard_map(
        body,
        mesh=mesh,
        in_specs=(
            P("dom", "aux", None, None),
            P("dom", None, None, None),
            P(),
            P(),
            P("dom", "aux", None),
        ),
        out_specs=P("dom", None, None),
        check_vma=False,
    )
```

```python
import jax
import jax.numpy as jnp
from jax import lax
from jax.experimental import pallas as pl
from jax.experimental.pallas import tpu as pltpu
from jax.sharding import PartitionSpec as P


RAD = 2
X_LEN, Z_LEN = 4, 8


def passed_along(block, axis, distance):
    devices = range(lax.axis_size(axis))
    route = [((i - distance) % len(devices), i) for i in devices]
    return lax.ppermute(block, axis, route)


def from_grid(block, dx, dz):
    route = []
    for x in range(X_LEN):
        for z in range(Z_LEN):
            source = (x - dx) % X_LEN * Z_LEN + (z - dz) % Z_LEN
            route.append((source, x * Z_LEN + z))
    return lax.ppermute(block, "aux", route)


def groups_along(which):
    lines = [[x * Z_LEN + z for z in range(Z_LEN)] for x in range(X_LEN)]
    return lines if which == "z" else [list(line) for line in zip(*lines)]


def to_all(copies, which):
    return lax.all_to_all(
        copies, "aux", split_axis=0, concat_axis=0, tiled=True,
        axis_index_groups=groups_along(which),
    )


def metric_kernel(me_ref, rows_ref, out_ref):
    kept = out_ref.shape[1]
    side = rows_ref.shape[1] // X_LEN
    my_x = me_ref[0] // Z_LEN
    for k in range(kept // side):
        place = lax.rem(my_x + k, X_LEN)
        out_ref[:, k * side:(k + 1) * side] = (
            rows_ref[:, pl.ds(pl.multiple_of(place * side, side), side)]
        )


def line_kernel(me_ref, *refs):
    *piece_refs, line_ref, short_ref = refs
    count = piece_refs[0].shape[0]
    my_z = lax.rem(me_ref[0], Z_LEN)
    for k, piece_ref in enumerate(piece_refs):
        place = lax.rem(my_z + (Z_LEN - k), Z_LEN)
        rows = pl.ds(pl.multiple_of(place * count, count), count)
        line_ref[rows, :] = piece_ref[...]
        short_ref[rows, :] = piece_ref[:, :short_ref.shape[1]]


def in_vmem(kernel, shapes, me, *arrays):
    whole = pl.BlockSpec(memory_space=pltpu.VMEM)
    return pl.pallas_call(
        kernel,
        out_shape=[jax.ShapeDtypeStruct(shape, arrays[0].dtype) for shape in shapes],
        in_specs=[pl.BlockSpec(memory_space=pltpu.SMEM)] + [whole] * len(arrays),
        out_specs=[whole] * len(shapes),
        compiler_params=pltpu.CompilerParams(vmem_limit_bytes=4 << 20),
    )(me, *arrays)


BLOCKS = {
    (0, 0): (0, 0), (0, 1): (0, 1), (0, 2): (0, 2),
    (1, 1): (1, 0), (1, 2): (1, 1), (1, 3): (1, 2),
    (2, 2): (2, 0), (2, 3): (2, 1),
    (3, 3): (3, 0), (3, 0): (3, 1),
}


def fit_kernel(me_ref, *refs):
    *metric_refs, ints_ref, out_ref = refs
    parts, width, depth, cols = ints_ref.shape
    count = len(metric_refs)
    share = parts // count
    block = share * depth
    my_x = me_ref[0] // share
    columns = []
    for k in range(count):
        place = lax.rem(my_x + k, count)
        tile = ints_ref[pl.ds(pl.multiple_of(place * share, share), share)]
        columns.append(jnp.concatenate(
            [tile[:, w].reshape(block, cols).T for w in range(width)], axis=0
        ))
    for q in range(count):
        total = jnp.zeros((width * cols, block), jnp.float32)
        for p in range(count):
            stored = (q, p) in BLOCKS
            piece, place = BLOCKS[(q, p) if stored else (p, q)]
            right = metric_refs[piece][:, place * block:(place + 1) * block]
            total += lax.dot_general(
                columns[p], right, (((1,), (1 if stored else 0,)), ((), ())),
                preferred_element_type=jnp.float32,
            )
        total = total.astype(out_ref.dtype)
        place = lax.rem(my_x + q, count)
        for w in range(width):
            out_ref[w, :, pl.ds(pl.multiple_of(place * block, block), block)] = (
                total[w * cols:(w + 1) * cols]
            )


def fit(metric_parts, me, ints, first, slots):
    parts, _, depth, cols = ints.shape
    width = 2
    rows = parts * depth
    return pl.pallas_call(
        fit_kernel,
        out_shape=jax.ShapeDtypeStruct((slots, cols, rows), ints.dtype),
        grid_spec=pltpu.PrefetchScalarGridSpec(
            num_scalar_prefetch=1,
            grid=(slots // width,),
            in_specs=[
                pl.BlockSpec(part.shape, lambda i, me: (0, 0)) for part in metric_parts
            ] + [
                pl.BlockSpec(
                    (parts, width, depth, cols),
                    lambda i, me: (0, i + first // width, 0, 0),
                ),
            ],
            out_specs=pl.BlockSpec((width, cols, rows), lambda i, me: (i, 0, 0)),
        ),
        compiler_params=pltpu.CompilerParams(vmem_limit_bytes=12 << 20),
        cost_estimate=pl.CostEstimate(
            flops=2 * rows * rows * slots * cols,
            bytes_accessed=2 * rows * rows + 4 * rows * slots * cols,
            transcendentals=0,
        ),
    )(me, *metric_parts, ints)


def close_kernel(most_ref, rest_ref, half_ref, out_ref, half_buf, rest_buf, sems):
    chunks, parts, width, depth, cols = half_buf.shape
    copies = [
        pltpu.make_async_copy(
            half_ref.at[:, pl.ds(width * c, width)], half_buf.at[c], sems.at[c],
        )
        for c in range(chunks)
    ]
    copies.append(pltpu.make_async_copy(rest_ref, rest_buf, sems.at[chunks]))
    for copy in copies:
        copy.start()
    kept = most_ref.shape[0]
    total = jnp.zeros((cols, cols), jnp.float32)
    for c in range(chunks):
        copies[c].wait()
        slots = range(width * c, width * (c + 1))
        if kept in slots:
            copies[chunks].wait()
        lefts = [most_ref[s] if s < kept else rest_buf[s - kept] for s in slots]
        rights = [half_buf[c, :, v].reshape(parts * depth, cols) for v in range(width)]
        both = jnp.dot(
            jnp.concatenate(lefts, axis=0), jnp.concatenate(rights, axis=1),
            preferred_element_type=jnp.float32,
        )
        total += both[:cols, :cols] + both[cols:, cols:]
    done = total.T.astype(out_ref.dtype)
    for k in range(out_ref.shape[0]):
        out_ref[k] = done


def close(most, rest, half):
    parts, slots, depth, cols = half.shape
    width = 2
    chunks = slots // width
    vmem, hbm = pltpu.VMEM, pltpu.HBM
    return pl.pallas_call(
        close_kernel,
        out_shape=jax.ShapeDtypeStruct((Z_LEN, cols, cols), half.dtype),
        in_specs=[pl.BlockSpec(memory_space=space) for space in (vmem, hbm, hbm)],
        out_specs=pl.BlockSpec(memory_space=vmem),
        scratch_shapes=[
            pltpu.VMEM((chunks, parts, width, depth, cols), half.dtype),
            pltpu.VMEM(rest.shape, rest.dtype),
            pltpu.SemaphoreType.DMA((chunks + 1,)),
        ],
        compiler_params=pltpu.CompilerParams(vmem_limit_bytes=16 << 20),
        cost_estimate=pl.CostEstimate(
            flops=2 * parts * depth * slots * cols * cols,
            bytes_accessed=4 * parts * depth * slots * cols,
            transcendentals=0,
        ),
    )(most, *(pltpu.with_memory_space_constraint(x, hbm) for x in (rest, half)))


def swap_kernel(in_ref, out_ref, in_buf, out_buf, in_sems, out_sems):
    chunks, _, width, _ = in_buf.shape
    reads, writes = [], []
    for c in range(chunks):
        slots = pl.ds(c * width, width)
        reads.append(pltpu.make_async_copy(in_ref.at[:, slots], in_buf.at[c], in_sems.at[c]))
        writes.append(pltpu.make_async_copy(out_buf.at[c], out_ref.at[slots], out_sems.at[c]))
    for read in reads:
        read.start()
    for c in range(chunks):
        reads[c].wait()
        out_buf[c] = jnp.swapaxes(in_buf[c], 0, 1)
        writes[c].start()
    for write in writes:
        write.wait()


def slot_major(array, chunks):
    count, slots, cols = array.shape
    width = slots // chunks
    return pl.pallas_call(
        swap_kernel,
        out_shape=pltpu.HBM((slots, count, cols), array.dtype),
        in_specs=[pl.BlockSpec(memory_space=pltpu.HBM)],
        out_specs=pl.BlockSpec(memory_space=pltpu.HBM),
        scratch_shapes=[
            pltpu.VMEM((chunks, count, width, cols), array.dtype),
            pltpu.VMEM((chunks, width, count, cols), array.dtype),
            pltpu.SemaphoreType.DMA((chunks,)),
            pltpu.SemaphoreType.DMA((chunks,)),
        ],
        compiler_params=pltpu.CompilerParams(vmem_limit_bytes=16 << 20),
        cost_estimate=pl.CostEstimate(
            flops=0, bytes_accessed=4 * array.size, transcendentals=0,
        ),
    )(pltpu.with_memory_space_constraint(array, pltpu.HBM))


def local_density(density, dens_cols, neighbours):
    domain_count = lax.axis_size("dom")
    my_domain = lax.axis_index("dom")
    block_size = density.shape[2]
    neigh_count = neighbours.shape[1]
    my_blocks = lax.dynamic_index_in_dim(neighbours, my_domain, 0, keepdims=False)
    slabs = []
    for offset in range(-RAD, RAD + 1):
        slabs.append(density[0] if offset == 0 else passed_along(density, "dom", -offset)[0])
    row_slabs = jnp.stack(slabs)
    slot_index = (my_blocks - my_domain + RAD) % domain_count
    picked = jnp.take(row_slabs, slot_index, axis=0)
    tile_cols = jnp.take(dens_cols, my_blocks, axis=0)
    matches = (tile_cols[:, None, :] == my_blocks[None, :, None]).astype(jnp.bfloat16)
    tiles = jnp.einsum("jsk,jkab->jasb", matches, picked, preferred_element_type=jnp.float32)
    order = neigh_count * block_size
    return tiles.astype(jnp.bfloat16).reshape(order, order)


def by_slot(array):
    group = lax.axis_size("aux")
    count, slots, cols = array.shape
    return array.transpose(1, 0, 2).reshape(group, slots // group, count, cols)


def exchanged(array):
    return lax.all_to_all(array, "aux", split_axis=0, concat_axis=0, tiled=True)


def body(integrals, density, dens_cols, neighbours, metric):
    ints, rows = integrals[0], metric[0]
    cols = ints.shape[2]
    count, side = rows.shape[0], rows.shape[1] // X_LEN
    me = lax.axis_index("aux")[None]
    ints_out = slot_major(ints, 16)
    group = lax.axis_size("aux")
    ints_moved = exchanged(ints_out.reshape(group, -1, count, cols))
    kept, = in_vmem(metric_kernel, [(count, 3 * side)], me, rows)
    pieces = [kept] + [from_grid(kept, 0, k) for k in range(1, Z_LEN)]
    dense = local_density(density, dens_cols, neighbours)
    half = jnp.einsum("ls,plm->psm", dense, ints, preferred_element_type=jnp.float32)
    half_moved = exchanged(by_slot(half.astype(jnp.bfloat16)))
    shapes = [(Z_LEN * count, 3 * side), (Z_LEN * count, 2 * side)]
    line, short = in_vmem(line_kernel, shapes, me, *pieces)
    parts = [line, from_grid(line, -1, 0), from_grid(short, 2, 0), from_grid(short, 1, 0)]
    most = 3 * ints_moved.shape[1] // 4
    rest = fit(parts, me, ints_moved, most, ints_moved.shape[1] - most)
    shares = close(fit(parts, me, ints_moved, 0, most), rest, half_moved)
    shares = jnp.sum(to_all(shares, "z").astype(jnp.float32), axis=0)
    shares = jnp.broadcast_to(shares[None], (X_LEN, cols, cols))
    return jnp.sum(to_all(shares, "x"), axis=0)[None]


def solution(mesh):
    return jax.shard_map(
        body,
        mesh=mesh,
        in_specs=(
            P("dom", "aux", None, None),
            P("dom", None, None, None),
            P(),
            P(),
            P("dom", "aux", None),
        ),
        out_specs=P("dom", None, None),
        check_vma=False,
    )
```

```python
import jax
import jax.numpy as jnp
from jax import lax
from jax.experimental import pallas as pl
from jax.experimental.pallas import tpu as pltpu
from jax.sharding import PartitionSpec as P


RAD = 2
X_LEN, Z_LEN = 4, 8


def passed_along(block, axis, distance):
    devices = range(lax.axis_size(axis))
    route = [((i - distance) % len(devices), i) for i in devices]
    return lax.ppermute(block, axis, route)


def from_grid(block, dx, dz):
    route = []
    for x in range(X_LEN):
        for z in range(Z_LEN):
            source = (x - dx) % X_LEN * Z_LEN + (z - dz) % Z_LEN
            route.append((source, x * Z_LEN + z))
    return lax.ppermute(block, "aux", route)


def groups_along(which):
    lines = [[x * Z_LEN + z for z in range(Z_LEN)] for x in range(X_LEN)]
    return lines if which == "z" else [list(line) for line in zip(*lines)]


def to_all(copies, which):
    return lax.all_to_all(
        copies, "aux", split_axis=0, concat_axis=0, tiled=True,
        axis_index_groups=groups_along(which),
    )


def metric_kernel(me_ref, rows_ref, out_ref):
    kept = out_ref.shape[1]
    side = rows_ref.shape[1] // X_LEN
    my_x = me_ref[0] // Z_LEN
    for k in range(kept // side):
        place = lax.rem(my_x + k, X_LEN)
        out_ref[:, k * side:(k + 1) * side] = (
            rows_ref[:, pl.ds(pl.multiple_of(place * side, side), side)]
        )


def line_kernel(me_ref, *refs):
    *piece_refs, line_ref, short_ref = refs
    count = piece_refs[0].shape[0]
    my_z = lax.rem(me_ref[0], Z_LEN)
    for k, piece_ref in enumerate(piece_refs):
        place = lax.rem(my_z + (Z_LEN - k), Z_LEN)
        rows = pl.ds(pl.multiple_of(place * count, count), count)
        line_ref[rows, :] = piece_ref[...]
        short_ref[rows, :] = piece_ref[:, :short_ref.shape[1]]


def in_vmem(kernel, shapes, me, *arrays):
    whole = pl.BlockSpec(memory_space=pltpu.VMEM)
    return pl.pallas_call(
        kernel,
        out_shape=[jax.ShapeDtypeStruct(shape, arrays[0].dtype) for shape in shapes],
        in_specs=[pl.BlockSpec(memory_space=pltpu.SMEM)] + [whole] * len(arrays),
        out_specs=[whole] * len(shapes),
        compiler_params=pltpu.CompilerParams(vmem_limit_bytes=4 << 20),
    )(me, *arrays)


BLOCKS = {
    (0, 0): (0, 0), (0, 1): (0, 1), (0, 2): (0, 2),
    (1, 1): (1, 0), (1, 2): (1, 1), (1, 3): (1, 2),
    (2, 2): (2, 0), (2, 3): (2, 1),
    (3, 3): (3, 0), (3, 0): (3, 1),
}


def fit_kernel(me_ref, *refs):
    *metric_refs, ints_ref, out_ref = refs
    parts, width, depth, cols = ints_ref.shape
    count = len(metric_refs)
    share = parts // count
    block = share * depth
    my_x = me_ref[0] // share
    columns = []
    for k in range(count):
        place = lax.rem(my_x + k, count)
        tile = ints_ref[pl.ds(pl.multiple_of(place * share, share), share)]
        columns.append(jnp.concatenate(
            [tile[:, w].reshape(block, cols).T for w in range(width)], axis=0
        ))
    for q in range(count):
        total = jnp.zeros((width * cols, block), jnp.float32)
        for p in range(count):
            stored = (q, p) in BLOCKS
            piece, place = BLOCKS[(q, p) if stored else (p, q)]
            right = metric_refs[piece][:, place * block:(place + 1) * block]
            total += lax.dot_general(
                columns[p], right, (((1,), (1 if stored else 0,)), ((), ())),
                preferred_element_type=jnp.float32,
            )
        total = total.astype(out_ref.dtype)
        place = lax.rem(my_x + q, count)
        for w in range(width):
            out_ref[w, :, pl.ds(pl.multiple_of(place * block, block), block)] = (
                total[w * cols:(w + 1) * cols]
            )


def fit(metric_parts, me, ints, first, slots):
    parts, _, depth, cols = ints.shape
    width = 2
    rows = parts * depth
    return pl.pallas_call(
        fit_kernel,
        out_shape=jax.ShapeDtypeStruct((slots, cols, rows), ints.dtype),
        grid_spec=pltpu.PrefetchScalarGridSpec(
            num_scalar_prefetch=1,
            grid=(slots // width,),
            in_specs=[
                pl.BlockSpec(part.shape, lambda i, me: (0, 0)) for part in metric_parts
            ] + [
                pl.BlockSpec(
                    (parts, width, depth, cols),
                    lambda i, me: (0, i + first // width, 0, 0),
                ),
            ],
            out_specs=pl.BlockSpec((width, cols, rows), lambda i, me: (i, 0, 0)),
        ),
        compiler_params=pltpu.CompilerParams(vmem_limit_bytes=12 << 20),
        cost_estimate=pl.CostEstimate(
            flops=2 * rows * rows * slots * cols,
            bytes_accessed=2 * rows * rows + 4 * rows * slots * cols,
            transcendentals=0,
        ),
    )(me, *metric_parts, ints)


def close_kernel(most_ref, rest_ref, half_ref, out_ref, half_buf, rest_buf, sems):
    chunks, parts, width, depth, cols = half_buf.shape
    copies = [
        pltpu.make_async_copy(
            half_ref.at[:, pl.ds(width * c, width)], half_buf.at[c], sems.at[c],
        )
        for c in range(chunks)
    ]
    copies.append(pltpu.make_async_copy(rest_ref, rest_buf, sems.at[chunks]))
    for copy in copies:
        copy.start()
    total = jnp.zeros((cols, cols), jnp.float32)
    for c in range(chunks):
        copies[c].wait()
        if c == chunks - 1:
            copies[chunks].wait()
        for w in range(0, width, 2):
            slots = (w, w + 1)
            if c < chunks - 1:
                lefts = [most_ref[width * c + v] for v in slots]
            else:
                lefts = [rest_buf[v] for v in slots]
            rights = [half_buf[c, :, v].reshape(parts * depth, cols) for v in slots]
            both = jnp.dot(
                jnp.concatenate(lefts, axis=0), jnp.concatenate(rights, axis=1),
                preferred_element_type=jnp.float32,
            )
            total += both[:cols, :cols] + both[cols:, cols:]
    done = total.T
    for k in range(out_ref.shape[0]):
        out_ref[k] = done


def close(most, rest, half):
    parts, slots, depth, cols = half.shape
    width = rest.shape[0]
    chunks = slots // width
    vmem, hbm = pltpu.VMEM, pltpu.HBM
    return pl.pallas_call(
        close_kernel,
        out_shape=jax.ShapeDtypeStruct((X_LEN, cols, cols), jnp.float32),
        in_specs=[pl.BlockSpec(memory_space=space) for space in (vmem, hbm, hbm)],
        out_specs=pl.BlockSpec(memory_space=vmem),
        scratch_shapes=[
            pltpu.VMEM((chunks, parts, width, depth, cols), half.dtype),
            pltpu.VMEM(rest.shape, rest.dtype),
            pltpu.SemaphoreType.DMA((chunks + 1,)),
        ],
        compiler_params=pltpu.CompilerParams(vmem_limit_bytes=16 << 20),
        cost_estimate=pl.CostEstimate(
            flops=2 * parts * depth * slots * cols * cols,
            bytes_accessed=4 * parts * depth * slots * cols,
            transcendentals=0,
        ),
    )(most, *(pltpu.with_memory_space_constraint(x, hbm) for x in (rest, half)))


def swap_kernel(in_ref, out_ref, in_buf, out_buf, in_sems, out_sems):
    chunks, _, width, _ = in_buf.shape
    reads, writes = [], []
    for c in range(chunks):
        slots = pl.ds(c * width, width)
        reads.append(pltpu.make_async_copy(in_ref.at[:, slots], in_buf.at[c], in_sems.at[c]))
        writes.append(pltpu.make_async_copy(out_buf.at[c], out_ref.at[slots], out_sems.at[c]))
    for read in reads:
        read.start()
    for c in range(chunks):
        reads[c].wait()
        out_buf[c] = jnp.swapaxes(in_buf[c], 0, 1)
        writes[c].start()
    for write in writes:
        write.wait()


def slot_major(array, chunks):
    count, slots, cols = array.shape
    width = slots // chunks
    return pl.pallas_call(
        swap_kernel,
        out_shape=pltpu.HBM((slots, count, cols), array.dtype),
        in_specs=[pl.BlockSpec(memory_space=pltpu.HBM)],
        out_specs=pl.BlockSpec(memory_space=pltpu.HBM),
        scratch_shapes=[
            pltpu.VMEM((chunks, count, width, cols), array.dtype),
            pltpu.VMEM((chunks, width, count, cols), array.dtype),
            pltpu.SemaphoreType.DMA((chunks,)),
            pltpu.SemaphoreType.DMA((chunks,)),
        ],
        compiler_params=pltpu.CompilerParams(vmem_limit_bytes=16 << 20),
        cost_estimate=pl.CostEstimate(
            flops=0, bytes_accessed=4 * array.size, transcendentals=0,
        ),
    )(pltpu.with_memory_space_constraint(array, pltpu.HBM))


def local_density(density, dens_cols, neighbours):
    domain_count = lax.axis_size("dom")
    my_domain = lax.axis_index("dom")
    block_size = density.shape[2]
    neigh_count = neighbours.shape[1]
    my_blocks = lax.dynamic_index_in_dim(neighbours, my_domain, 0, keepdims=False)
    slabs = []
    for offset in range(-RAD, RAD + 1):
        slabs.append(density[0] if offset == 0 else passed_along(density, "dom", -offset)[0])
    row_slabs = jnp.stack(slabs)
    slot_index = (my_blocks - my_domain + RAD) % domain_count
    picked = jnp.take(row_slabs, slot_index, axis=0)
    tile_cols = jnp.take(dens_cols, my_blocks, axis=0)
    matches = (tile_cols[:, None, :] == my_blocks[None, :, None]).astype(jnp.bfloat16)
    tiles = jnp.einsum("jsk,jkab->jasb", matches, picked, preferred_element_type=jnp.float32)
    order = neigh_count * block_size
    return tiles.astype(jnp.bfloat16).reshape(order, order)


def by_slot(array):
    group = lax.axis_size("aux")
    count, slots, cols = array.shape
    return array.transpose(1, 0, 2).reshape(group, slots // group, count, cols)


def exchanged(array):
    return lax.all_to_all(array, "aux", split_axis=0, concat_axis=0, tiled=True)


def body(integrals, density, dens_cols, neighbours, metric):
    ints, rows = integrals[0], metric[0]
    cols = ints.shape[2]
    count, side = rows.shape[0], rows.shape[1] // X_LEN
    me = lax.axis_index("aux")[None]
    ints_out = slot_major(ints, 4)
    group = lax.axis_size("aux")
    ints_moved = exchanged(ints_out.reshape(group, -1, count, cols))
    kept, = in_vmem(metric_kernel, [(count, 3 * side)], me, rows)
    pieces = [kept] + [from_grid(kept, 0, k) for k in range(1, Z_LEN)]
    dense = local_density(density, dens_cols, neighbours)
    half = jnp.einsum("ls,plm->psm", dense, ints, preferred_element_type=jnp.float32)
    half_moved = exchanged(by_slot(half.astype(jnp.bfloat16)))
    shapes = [(Z_LEN * count, 3 * side), (Z_LEN * count, 2 * side)]
    line, short = in_vmem(line_kernel, shapes, me, *pieces)
    parts = [line, from_grid(line, -1, 0), from_grid(short, 2, 0), from_grid(short, 1, 0)]
    most = 3 * ints_moved.shape[1] // 4
    rest = fit(parts, me, ints_moved, most, ints_moved.shape[1] - most)
    shares = close(fit(parts, me, ints_moved, 0, most), rest, half_moved)
    shares = jnp.sum(to_all(shares, "x"), axis=0).astype(jnp.bfloat16)
    shares = jnp.broadcast_to(shares[None], (Z_LEN, cols, cols))
    shares = to_all(shares, "z").astype(jnp.float32)
    return jnp.sum(shares, axis=0)[None]


def solution(mesh):
    return jax.shard_map(
        body,
        mesh=mesh,
        in_specs=(
            P("dom", "aux", None, None),
            P("dom", None, None, None),
            P(),
            P(),
            P("dom", "aux", None),
        ),
        out_specs=P("dom", None, None),
        check_vma=False,
    )
```
